32 devices in a mesh: ctx: 16 (over z, y, core), wsh: 2 (over x).
Axes of the slice: x: 2, y: 2, z: 4, core: 2. Of those that a mesh axis runs over, the one named last changes fastest.
Arguments:
- tokens: bfloat16 [4, 2048, 1024], P('wsh', 'ctx'), may hold values from -6 to 6
- segment_ids: int32 [4, 2048], P('wsh', 'ctx'), may hold values from 0 to 15, never falling along the last dimension, each value on 1 to 512 neighbouring positions
- cotangent: bfloat16 [4, 2048, 1024], P('wsh', 'ctx'), may hold values from -6 to 6
- qkv_master: float32 [1024, 2048], P('wsh', 'ctx'), may hold values from -0.1875 to 0.1875
- qkv_mean: float32 [1024, 2048], P('wsh', 'ctx'), may hold values from -27.1529 to 27.1529
- qkv_square: float32 [1024, 2048], P('wsh', 'ctx'), may hold values from 0.8192 to 13.1072
- proj_master: float32 [1024, 1024], P('wsh', 'ctx'), may hold values from -1.5 to 1.5
- proj_mean: float32 [1024, 1024], P('wsh', 'ctx'), may hold values from -27.1529 to 27.1529
- proj_square: float32 [1024, 1024], P('wsh', 'ctx'), may hold values from 0.8192 to 13.1072
- upgate_master: float32 [1024, 9216], P('wsh', 'ctx'), may hold values from -0.1875 to 0.1875
- upgate_mean: float32 [1024, 9216], P('wsh', 'ctx'), may hold values from -27.1529 to 27.1529
- upgate_square: float32 [1024, 9216], P('wsh', 'ctx'), may hold values from 0.8192 to 13.1072
- down_master: float32 [4608, 1024], P('wsh', 'ctx'), may hold values from -0.09375 to 0.09375
- down_mean: float32 [4608, 1024], P('wsh', 'ctx'), may hold values from -27.1529 to 27.1529
- down_square: float32 [4608, 1024], P('wsh', 'ctx'), may hold values from 0.8192 to 13.1072
- gain_master: float32 [2176], replicated, may hold values from 0.5 to 1.5
- gain_mean: float32 [2176], replicated, may hold values from -27.1529 to 27.1529
- gain_square: float32 [2176], replicated, may hold values from 0.8192 to 13.1072
Outputs:
- block_out: bfloat16 [4, 2048, 1024], P('wsh', 'ctx')
- input_grad: float32 [4, 2048, 1024], P('wsh', 'ctx')
- qkv_grad: float32 [1024, 2048], P('wsh', 'ctx')
- qkv_weight: float32 [1024, 2048], P('wsh', 'ctx')
- qkv_first: float32 [1024, 2048], P('wsh', 'ctx')
- qkv_second: float32 [1024, 2048], P('wsh', 'ctx')
- proj_grad: float32 [1024, 1024], P('wsh', 'ctx')
- proj_weight: float32 [1024, 1024], P('wsh', 'ctx')
- proj_first: float32 [1024, 1024], P('wsh', 'ctx')
- proj_second: float32 [1024, 1024], P('wsh', 'ctx')
- upgate_grad: float32 [1024, 9216], P('wsh', 'ctx')
- upgate_weight: float32 [1024, 9216], P('wsh', 'ctx')
- upgate_first: float32 [1024, 9216], P('wsh', 'ctx')
- upgate_second: float32 [1024, 9216], P('wsh', 'ctx')
- down_grad: float32 [4608, 1024], P('wsh', 'ctx')
- down_weight: float32 [4608, 1024], P('wsh', 'ctx')
- down_first: float32 [4608, 1024], P('wsh', 'ctx')
- down_second: float32 [4608, 1024], P('wsh', 'ctx')
- gain_grad: float32 [2176], replicated
- gain_weight: float32 [2176], replicated
- gain_first: float32 [2176], replicated
- gain_second: float32 [2176], replicated
- lamb_norms: float32 [2, 8], replicated
The draws below stay inside these ranges and needn't reach their ends.
Inputs may be any that keep to these rules, and one draw needn't show every extreme that they name: `segment_ids`: in each sequence the numbers never fall; a sequence holds 16 documents of 1 to 512 tokens, one of exactly 512 tokens.
All inputs are finite; a program needn't handle non-finite values.
Results may differ from the reference program's by a relative error of at most 0.02.
Values may be sent and summed in bfloat16 or wider, within the bound.
No kernel may reach another device: no remote copies, remote signals or barrier semaphores. Data moves between devices by JAX's collectives and lax.ppermute only.
A program may use at most 192 MiB of HBM per device.

```python
import math
import jax
import jax.numpy as jnp
import numpy as np
from jax import lax

D = 1024
QUERY_HEADS = 16
KEY_VALUE_HEADS = 8
HEAD_WIDTH = 64
FF = 4608
DOCS = 16
STEP = 10
QKV = 2048
GAINS = 2176
SEQUENCE_LENGTH = 2048
NSEQ = 4


def raised(result, rng, source, target, shards_of, factor):
    owner, partner = [(jnp.arange(result.shape[axis_at]) // (result.shape[axis_at] // shards_of)).reshape([-1 if axis == axis_at else 1 for axis in range(result.ndim)]) for axis_at in (source, target)]
    chosen = jax.random.permutation(rng, shards_of)[partner]
    strong = (owner == chosen) | (owner == (partner + shards_of // 2) % shards_of)
    return jnp.where(strong, factor * result, result)


def shard_levels(own_key, extent, cuts, low, top_value):
    level, own = 1.0, jax.random.fold_in(own_key, 6)
    for position, blocks in cuts:
        heights = jnp.exp(jax.random.uniform(jax.random.fold_in(own, position), (blocks,), jnp.float32, low / len(cuts), top_value / len(cuts)))
        level = level * jnp.repeat(heights, extent[position] // blocks).reshape([-1 if axis == position else 1 for axis in range(len(extent))])
    return level


def profile(number_of, total, most, skew):
    loads = [(1 << 20) // math.isqrt(rank ** skew) + 1 for rank in range(2, number_of + 1)]
    rest, holding = total - most - (number_of - 1), [1] * (number_of - 1)
    while rest > 0:
        free = [i for i in range(number_of - 1) if holding[i] < most]
        mass, remaining = sum([loads[i] for i in free]), rest
        for i in free:
            extra = min(most - holding[i], max(1, remaining * loads[i] // mass), rest)
            holding[i] = holding[i] + extra
            rest = rest - extra
    return np.array([most] + holding)


def ragged(rng, number_of, total, bound, slope):
    if number_of == 2:
        one = jax.random.randint(rng, (), max(1, total - bound), min(bound, total - 1) + 1)
        return jnp.stack([one, total - one])
    lengths = jnp.asarray(profile(number_of, total, bound, slope), jnp.int32)
    pairs = (number_of - 1) // 2
    giver, sink = lengths[1:1 + 2 * pairs:2], lengths[2:2 + 2 * pairs:2]
    slack = jnp.minimum(giver - 1, bound - sink)
    passed = jax.random.randint(jax.random.fold_in(rng, 1), (pairs,), 0, 1 << 20) % (slack + 1)
    lengths = lengths.at[1:1 + 2 * pairs:2].set(giver - passed).at[2:2 + 2 * pairs:2].set(sink + passed)
    return lengths[jax.random.permutation(jax.random.fold_in(rng, 2), number_of)]


def centred(stream_key, shape, width, bound, shards=(), held_as=jnp.bfloat16):
    result = jax.random.normal(stream_key, shape, jnp.float32) * width
    if len(shards) > 0:
        result = shard_levels(stream_key, shape, shards, -0.22, 0.18) * result
    return jnp.clip(result, min=-bound, max=bound).astype(held_as)


def noise_with(rng, extent, spread, reach, split, heavy, held_as=jnp.bfloat16):
    values = spread * jax.random.normal(rng, extent, jnp.float32)
    if split:
        values = values * shard_levels(rng, extent, split, -0.22, 0.18)
    return jnp.clip(raised(values, jax.random.fold_in(rng, 3), *heavy), -reach, reach).astype(held_as)


def setup_inputs(seed: int = 0) -> dict:
    seeds = jax.random.split(jax.random.key(seed), 19)
    tokens = centred(seeds[0], (NSEQ, SEQUENCE_LENGTH, D), 1.0, 6.0, ((0, 2), (1, 16)))
    segment_ids = jax.vmap(lambda own: jnp.searchsorted(jnp.cumsum(ragged(own, DOCS, SEQUENCE_LENGTH, SEQUENCE_LENGTH // 4, 2)), jnp.arange(SEQUENCE_LENGTH), side="right"))(jax.random.split(seeds[1], NSEQ)).reshape((NSEQ, SEQUENCE_LENGTH)).astype(jnp.int32)
    cotangent = noise_with(seeds[2], (NSEQ, SEQUENCE_LENGTH, D), 1.0, 6.0, ((0, 2), (1, 16)), (1, 2, 16, 2.0))
    qkv_master = centred(seeds[3], (D, QKV), D ** -0.5, 0.1875, ((0, 2), (1, 16)), jnp.float32)
    qkv_mean = centred(seeds[4], (D, QKV), (0.05 * (NSEQ * SEQUENCE_LENGTH) ** 0.5), 27.1529, ((0, 2), (1, 16)), jnp.float32)
    qkv_square = jnp.clip(jnp.exp(math.log(13.1072) - 2.7725887 * jax.random.uniform(seeds[5], (D, QKV), jnp.float32) ** shard_levels(seeds[5], (D, QKV), ((0, 2), (1, 16)), -0.2, 0.2)), 0.8192, 13.1072)
    proj_master = centred(seeds[6], (D, D), (D // 64) ** -0.5, 1.5, ((0, 2), (1, 16)), jnp.float32)
    proj_mean = centred(seeds[7], (D, D), (0.05 * (NSEQ * SEQUENCE_LENGTH) ** 0.5), 27.1529, ((0, 2), (1, 16)), jnp.float32)
    proj_square = jnp.clip(jnp.exp(math.log(13.1072) - 2.7725887 * jax.random.uniform(seeds[8], (D, D), jnp.float32) ** shard_levels(seeds[8], (D, D), ((0, 2), (1, 16)), -0.2, 0.2)), 0.8192, 13.1072)
    upgate_master = centred(seeds[9], (D, 2 * FF), D ** -0.5, 0.1875, ((0, 2), (1, 16)), jnp.float32)
    upgate_mean = centred(seeds[10], (D, 2 * FF), (0.05 * (NSEQ * SEQUENCE_LENGTH) ** 0.5), 27.1529, ((0, 2), (1, 16)), jnp.float32)
    upgate_square = jnp.clip(jnp.exp(math.log(13.1072) - 2.7725887 * jax.random.uniform(seeds[11], (D, 2 * FF), jnp.float32) ** shard_levels(seeds[11], (D, 2 * FF), ((0, 2), (1, 16)), -0.2, 0.2)), 0.8192, 13.1072)
    down_master = centred(seeds[12], (FF, D), FF ** -0.5, 0.09375, ((0, 2), (1, 16)), jnp.float32)
    down_mean = centred(seeds[13], (FF, D), (0.05 * (NSEQ * SEQUENCE_LENGTH) ** 0.5), 27.1529, ((0, 2), (1, 16)), jnp.float32)
    down_square = jnp.clip(jnp.exp(math.log(13.1072) - 2.7725887 * jax.random.uniform(seeds[14], (FF, D), jnp.float32) ** shard_levels(seeds[14], (FF, D), ((0, 2), (1, 16)), -0.2, 0.2)), 0.8192, 13.1072)
    gain_master = jnp.clip(1.0 + 0.1 * jax.random.normal(seeds[15], (GAINS,), jnp.float32), 0.5, 1.5)
    gain_mean = centred(seeds[16], (GAINS,), (0.05 * (NSEQ * SEQUENCE_LENGTH) ** 0.5), 27.1529, (), jnp.float32)
    gain_square = jnp.clip(jnp.exp(jax.random.uniform(seeds[17], (GAINS,), jnp.float32, math.log(0.8192), math.log(13.1072))), 0.8192, 13.1072)
    return dict(tokens=tokens, segment_ids=segment_ids, cotangent=cotangent, qkv_master=qkv_master, qkv_mean=qkv_mean, qkv_square=qkv_square, proj_master=proj_master, proj_mean=proj_mean, proj_square=proj_square, upgate_master=upgate_master, upgate_mean=upgate_mean, upgate_square=upgate_square, down_master=down_master, down_mean=down_mean, down_square=down_square, gain_master=gain_master, gain_mean=gain_mean, gain_square=gain_square)


@jax.custom_vjp
def low(v):
    return lax.optimization_barrier(v.astype(jnp.bfloat16)).astype(jnp.float32)

@jax.custom_vjp
def low_back(v):
    return v

def low_keep(v):
    return (low(v), None)

def low_pass(kept, grad):
    return (grad,)

def back_keep(v):
    return (v, None)

def back_low(kept, grad):
    return (low(grad),)
low.defvjp(low_keep, low_pass)
low_back.defvjp(back_keep, back_low)
EPS_NORM = 1e-05
BETA_ONE = 0.9
BETA_TWO = 0.999
EPS_ADAM = 1e-06
DECAY = 0.01
RATE = 0.5
NEGATIVE_FILLER = -1e+30
HIGH = lax.Precision.HIGHEST

def rms_norm(inputs, gain):
    return inputs * lax.rsqrt(lax.optimization_barrier(jnp.mean(inputs * inputs, axis=-1, keepdims=True)) + EPS_NORM) * gain

def attend(queries, keys, values, segs):
    query_groups = QUERY_HEADS // KEY_VALUE_HEADS
    keys_all = jnp.repeat(keys, query_groups, axis=1)
    values_all = jnp.repeat(values, query_groups, axis=1)
    block = min(512, SEQUENCE_LENGTH)
    positions = jnp.arange(SEQUENCE_LENGTH, dtype=jnp.int32)

    def one_block(start):
        query_blk = lax.dynamic_slice_in_dim(queries, start, block, 0)
        query_seg = lax.dynamic_slice_in_dim(segs, start, block, 0)
        query_pos = start + jnp.arange(block, dtype=jnp.int32)
        raw = low_back(jnp.einsum('ihd,jhd->hij', query_blk, keys_all, precision=HIGH) * HEAD_WIDTH ** (-0.5))
        mask = (query_seg[:, None] == segs[None, :]) & (positions[None, :] <= query_pos[:, None])
        probs = jax.nn.softmax(jnp.where(mask, raw, NEGATIVE_FILLER), axis=-1)
        return jnp.einsum('hij,jhd->ihd', low(probs), values_all, precision=HIGH)
    starts = jnp.arange(SEQUENCE_LENGTH // block, dtype=jnp.int32) * block
    blocks = lax.map(jax.checkpoint(one_block), starts)
    return blocks.reshape(SEQUENCE_LENGTH, QUERY_HEADS * HEAD_WIDTH)

def layer(inputs, segs, weights, gains):
    qkv_weight, proj_weight, upgate_weight, down_weight = weights
    attn_gain = gains[:D]
    ffn_gain = gains[D:2 * D]
    query_gain = gains[2 * D:2 * D + HEAD_WIDTH]
    key_norm_scale = gains[2 * D + HEAD_WIDTH:]
    query_columns = QUERY_HEADS * HEAD_WIDTH
    key_columns = KEY_VALUE_HEADS * HEAD_WIDTH
    normed = low(rms_norm(inputs, attn_gain))
    projected_output = low_back(jnp.dot(normed, qkv_weight, precision=HIGH))
    q_raw = projected_output[:, :query_columns].reshape(SEQUENCE_LENGTH, QUERY_HEADS, HEAD_WIDTH)
    unnormed_key = projected_output[:, query_columns:query_columns + key_columns].reshape(SEQUENCE_LENGTH, KEY_VALUE_HEADS, HEAD_WIDTH)
    unnormed_value = projected_output[:, query_columns + key_columns:].reshape(SEQUENCE_LENGTH, KEY_VALUE_HEADS, HEAD_WIDTH)
    queries = low(rms_norm(q_raw, query_gain))
    keys = low(rms_norm(unnormed_key, key_norm_scale))
    values = low(unnormed_value)
    attended = low(low_back(attend(queries, keys, values, segs)))
    middle = inputs + low_back(jnp.dot(attended, proj_weight, precision=HIGH))
    normed_two = low(rms_norm(middle, ffn_gain))
    upgate = low_back(jnp.dot(normed_two, upgate_weight, precision=HIGH))
    hidden = low(jax.nn.silu(upgate[:, :FF]) * upgate[:, FF:])
    return middle + low_back(jnp.dot(hidden, down_weight, precision=HIGH))

def forward_all(masters, gains, inputs_all, segs_all):
    weights = (low(masters[0]), low(masters[1]), low(masters[2]), low(masters[3]))
    checked = jax.checkpoint(layer)

    def one_seq(bundle):
        return checked(bundle[0], bundle[1], weights, gains)
    return lax.map(one_seq, (inputs_all, segs_all))

def lamb_moments(grad, mean, square):
    first = BETA_ONE * mean + (1.0 - BETA_ONE) * grad
    second = BETA_TWO * square + (1.0 - BETA_TWO) * grad * grad
    bias_one = 1.0 - BETA_ONE ** STEP
    bias_two = 1.0 - BETA_TWO ** STEP
    direction = first / bias_one / (jnp.sqrt(second / bias_two) + EPS_ADAM)
    return (first, second, direction)

def reference(tokens, segment_ids, cotangent, qkv_master, qkv_mean, qkv_square, proj_master, proj_mean, proj_square, upgate_master, upgate_mean, upgate_square, down_master, down_mean, down_square, gain_master, gain_mean, gain_square):
    masters = (qkv_master, proj_master, upgate_master, down_master)
    means = (qkv_mean, proj_mean, upgate_mean, down_mean)
    squares = (qkv_square, proj_square, upgate_square, down_square)

    def forward(masters_in, gains_in, inputs_in):
        return forward_all(masters_in, gains_in, inputs_in, segment_ids)
    outputs, pullback = jax.vjp(forward, masters, gain_master, tokens.astype(jnp.float32))
    grad_masters, gain_grad, input_grad = pullback(cotangent.astype(jnp.float32))
    firsts = []
    seconds = []
    updates = []
    weight_sq = []
    update_sq = []
    for master, grad, mean, square in zip(masters, grad_masters, means, squares):
        first, second, direction = lamb_moments(grad, mean, square)
        update = direction + DECAY * master
        firsts.append(first)
        seconds.append(second)
        updates.append(update)
        weight_sq.append(jnp.sum(master * master))
        update_sq.append(jnp.sum(update * update))
    gain_first, gain_second, gain_update = lamb_moments(gain_grad, gain_mean, gain_square)
    bounds = [0, D, 2 * D, 2 * D + HEAD_WIDTH, GAINS]
    for index in range(4):
        piece_w = gain_master[bounds[index]:bounds[index + 1]]
        piece_u = gain_update[bounds[index]:bounds[index + 1]]
        weight_sq.append(jnp.sum(piece_w * piece_w))
        update_sq.append(jnp.sum(piece_u * piece_u))
    weight_norms = jnp.sqrt(jnp.stack(weight_sq))
    update_norms = jnp.sqrt(jnp.stack(update_sq))
    ratios = weight_norms / (update_norms + EPS_ADAM)
    new_weights = []
    for index in range(4):
        new_weights.append(masters[index] - RATE * ratios[index] * updates[index])
    ratio_vec = jnp.concatenate([jnp.full((D,), 1.0, jnp.float32) * ratios[4], jnp.full((D,), 1.0, jnp.float32) * ratios[5], jnp.full((HEAD_WIDTH,), 1.0, jnp.float32) * ratios[6], jnp.full((HEAD_WIDTH,), 1.0, jnp.float32) * ratios[7]])
    gain_weight = gain_master - RATE * ratio_vec * gain_update
    lamb_norms = jnp.stack([weight_norms, update_norms])
    return (outputs.astype(jnp.bfloat16), input_grad, grad_masters[0], new_weights[0], firsts[0], seconds[0], grad_masters[1], new_weights[1], firsts[1], seconds[1], grad_masters[2], new_weights[2], firsts[2], seconds[2], grad_masters[3], new_weights[3], firsts[3], seconds[3], gain_grad, gain_weight, gain_first, gain_second, lamb_norms)
```

```python
import functools

import jax
import jax.numpy as jnp
from jax import lax
from jax.experimental import pallas as pl
from jax.experimental.pallas import tpu as pltpu
from jax.sharding import Mesh
from jax.sharding import PartitionSpec as P

D = 1024
QUERY_HEADS = 16
KEY_VALUE_HEADS = 8
HEAD_WIDTH = 64
FF = 4608
STEP = 10
GAINS = 2176
QUERY_COLUMNS = QUERY_HEADS * HEAD_WIDTH
KEY_COLUMNS = KEY_VALUE_HEADS * HEAD_WIDTH
PAIR = 2 * HEAD_WIDTH
N_PAIRS = KEY_VALUE_HEADS // 2

EPS_NORM = 1e-05
BETA_ONE = 0.9
BETA_TWO = 0.999
EPS_ADAM = 1e-06
DECAY = 0.01
RATE = 0.5
NEGATIVE_FILLER = -1e30

BLK = ("far", "near")
CTX = ("far", "near", "core")
EVERY = ("far", "near", "core", "wsh")

BF = jnp.bfloat16
F32 = jnp.float32


def swap(block, axis):
    return lax.ppermute(block, axis, [(0, 1), (1, 0)])


def from_earlier(block, distance):
    n = lax.axis_size(CTX)
    return lax.ppermute(block, CTX, [(i - distance, i) for i in range(distance, n)])


def to_earlier(block, distance):
    n = lax.axis_size(CTX)
    return lax.ppermute(block, CTX, [(i, i - distance) for i in range(distance, n)])


def in_order(mine, other, index):
    return jnp.where(index == 0, jnp.stack([mine, other]), jnp.stack([other, mine]))


def pick(array, index, axis):
    return lax.dynamic_index_in_dim(array, index, axis, keepdims=False)


def total_everywhere(block):
    for axis in ("core", "wsh", "near", "far"):
        size = lax.axis_size(axis)
        step = 1
        while step < size:
            block = block + lax.ppermute(block, axis, [(i, i ^ step) for i in range(size)])
            step *= 2
    return block


def rms_norm(inputs, gain):
    inverse = lax.rsqrt(jnp.mean(inputs * inputs, axis=-1, keepdims=True) + EPS_NORM)
    return inputs * inverse * gain, inverse


def norm_back(inputs, inverse, gain, grad_out):
    weighted = grad_out * gain
    inner = jnp.mean(weighted * inputs, axis=-1, keepdims=True)
    grad_in = inverse * weighted - inputs * (inverse * inverse * inverse) * inner
    return grad_in, grad_out * inputs * inverse


def lamb_moments(grad, mean, square):
    first = BETA_ONE * mean + (1.0 - BETA_ONE) * grad
    second = BETA_TWO * square + (1.0 - BETA_TWO) * grad * grad
    bias_one = 1.0 - BETA_ONE**STEP
    bias_two = 1.0 - BETA_TWO**STEP
    direction = first / bias_one / (jnp.sqrt(second / bias_two) + EPS_ADAM)
    return first, second, direction


def low_half():
    return lax.broadcasted_iota(jnp.int32, (1, PAIR), 1) < HEAD_WIDTH


def half_sums(block):
    low = low_half()
    first = jnp.sum(jnp.where(low, block, 0.0), axis=-1, keepdims=True)
    second = jnp.sum(jnp.where(low, 0.0, block), axis=-1, keepdims=True)
    return jnp.where(low, first, second)


def head_norm(block, gain):
    inverse = lax.rsqrt(half_sums(block * block) * (1.0 / HEAD_WIDTH) + EPS_NORM)
    return block * inverse * gain, inverse


def spread(block):
    low = low_half()
    turned = pltpu.roll(block, HEAD_WIDTH, 1)
    return jnp.where(low, block, turned).astype(BF), jnp.where(low, turned, block).astype(BF)


def stacked(block):
    low = low_half()
    return jnp.concatenate([jnp.where(low, block, 0.0), jnp.where(low, 0.0, block)], axis=0).astype(BF)


def unstacked(block):
    rows = block.shape[0] // 2
    return jnp.where(low_half(), block[:rows], block[rows:])


def dot_nt(a, b):
    return lax.dot_general(a, b, (((1,), (1,)), ((), ())), preferred_element_type=F32)


def dot_tn(a, b):
    return lax.dot_general(a, b, (((0,), (0,)), ((), ())), preferred_element_type=F32)


def dot_nn(a, b):
    return lax.dot_general(a, b, (((1,), (0,)), ((), ())), preferred_element_type=F32)


def allowed_mask(q_seg, k_seg, rows, keys):
    behind = keys - rows
    row = lax.broadcasted_iota(jnp.int32, (rows, keys), 0)
    col = lax.broadcasted_iota(jnp.int32, (rows, keys), 1)
    mask = (q_seg == k_seg) & (col <= row + behind)
    return jnp.concatenate([mask, mask], axis=0)


def softmax_parts(scores, mask):
    filled = jnp.where(mask, scores, NEGATIVE_FILLER)
    top = jnp.max(filled, axis=-1, keepdims=True)
    weights = jnp.exp(filled - top)
    return weights, 1.0 / jnp.sum(weights, axis=-1, keepdims=True)


def forward_kernel(q_ref, k_ref, v_ref, qs_ref, ks_ref, gq_ref, gk_ref, o_ref):
    rows, keys = q_ref.shape[1], k_ref.shape[1]
    mask = allowed_mask(qs_ref[0], ks_ref[0], rows, keys)
    key_pair = spread(head_norm(k_ref[0], gk_ref[...])[0])
    value_pair = spread(v_ref[0])
    for head in range(2):
        at = pl.ds(head * PAIR, PAIR)
        query = head_norm(q_ref[0, :, at], gq_ref[...])[0].astype(BF).astype(F32)
        scores = dot_nt(stacked(query * HEAD_WIDTH**-0.5), key_pair[head])
        weights, inverse = softmax_parts(scores, mask)
        o_ref[0, :, at] = unstacked(dot_nn(weights.astype(BF), value_pair[head]) * inverse).astype(BF)


def backward_kernel(
    q_ref, k_ref, v_ref, go_ref, qs_ref, ks_ref, gq_ref, gk_ref,
    gq_out, gk_own, gv_own, gk_halo, gv_halo, gain_out,
):
    rows, keys = q_ref.shape[1], k_ref.shape[1]
    behind = keys - rows
    mask = allowed_mask(qs_ref[0], ks_ref[0], rows, keys)
    key_pair = spread(head_norm(k_ref[0], gk_ref[...])[0])
    value_pair = spread(v_ref[0])
    low = low_half()

    @pl.when((pl.program_id(0) == 0) & (pl.program_id(1) == 0))
    def _():
        gain_out[...] = jnp.zeros_like(gain_out)

    grad_keys, grad_values = [], []
    for head in range(2):
        at = pl.ds(head * PAIR, PAIR)
        raw = q_ref[0, :, at]
        normed, inverse_norm = head_norm(raw, gq_ref[...])
        query = stacked(normed.astype(BF).astype(F32) * HEAD_WIDTH**-0.5)
        scores = dot_nt(query, key_pair[head])
        weights, inverse = softmax_parts(scores, mask)
        probs = weights * inverse
        grad_out = stacked(go_ref[0, :, at].astype(F32))
        grad_probs = dot_nt(grad_out, value_pair[head])
        delta = jnp.sum(probs * grad_probs, axis=-1, keepdims=True)
        grad_scores = (probs * (grad_probs - delta)).astype(BF)
        grad_query = unstacked(dot_nn(grad_scores, key_pair[head])) * HEAD_WIDTH**-0.5
        key_part = dot_tn(grad_scores, query)
        value_part = dot_tn(probs.astype(BF), grad_out)
        grad_keys.append(key_part + pltpu.roll(key_part, HEAD_WIDTH, 1))
        grad_values.append(value_part + pltpu.roll(value_part, HEAD_WIDTH, 1))
        weighted = grad_query * gq_ref[...]
        inner = half_sums(weighted * raw) * (1.0 / HEAD_WIDTH)
        cubed = inverse_norm * inverse_norm * inverse_norm
        gq_out[0, :, at] = (inverse_norm * weighted - raw * cubed * inner).astype(BF)
        gain_out[0:1, :] += jnp.sum(grad_query * raw * inverse_norm, axis=0, keepdims=True)
    grad_key = jnp.where(low, grad_keys[0], grad_keys[1])
    grad_value = jnp.where(low, grad_values[0], grad_values[1])
    gk_own[0] = grad_key[behind:]
    gv_own[0] = grad_value[behind:]
    gk_halo[0] = grad_key[:behind].astype(BF)
    gv_halo[0] = grad_value[:behind].astype(BF)


def fold_kernel(depth, *refs):
    gk_own, gv_own = refs[0], refs[1]
    others = refs[2 : 2 + depth]
    k_ref, gk_ref, out, gain_out = refs[2 + depth :]
    gain = jnp.zeros((1, PAIR), F32)
    for pair in range(N_PAIRS):
        at = pl.ds(pair * PAIR, PAIR)
        at_v = pl.ds(KEY_COLUMNS + pair * PAIR, PAIR)
        grad_key, grad_value = gk_own[0, :, at], gv_own[0, :, at]
        for other in others:
            grad_key += other[0, :, at].astype(F32)
            grad_value += other[0, :, at_v].astype(F32)
        raw = k_ref[0, :, at]
        inverse = head_norm(raw, gk_ref[...])[1]
        weighted = grad_key * gk_ref[...]
        inner = half_sums(weighted * raw) * (1.0 / HEAD_WIDTH)
        out[0, :, at] = (inverse * weighted - raw * (inverse * inverse * inverse) * inner).astype(BF)
        out[0, :, at_v] = grad_value.astype(BF)
        gain += jnp.sum(grad_key * raw * inverse, axis=0, keepdims=True)
    gain_out[0] = gain


def attention_specs(rows, keys):
    q_spec = pl.BlockSpec((1, rows, 2 * PAIR), lambda s, p: (s, 0, p))
    k_spec = pl.BlockSpec((1, keys, PAIR), lambda s, p: (s, 0, p))
    v_spec = pl.BlockSpec((1, keys, PAIR), lambda s, p: (s, 0, N_PAIRS + p))
    qs_spec = pl.BlockSpec((1, rows, 1), lambda s, p: (s, 0, 0))
    ks_spec = pl.BlockSpec((1, 1, keys), lambda s, p: (s, 0, 0))
    gain_spec = pl.BlockSpec((1, PAIR), lambda s, p: (0, 0))
    return q_spec, k_spec, v_spec, qs_spec, ks_spec, gain_spec


def attention_cost(micro, rows, keys, products):
    work = micro * QUERY_HEADS * rows * keys
    return pl.CostEstimate(
        flops=2 * 4 * PAIR * products * work,
        bytes_accessed=micro * (rows * 6 * QUERY_COLUMNS + keys * 8 * KEY_COLUMNS),
        transcendentals=work,
    )


def attend(q, kv, q_seg, k_seg, gq, gk):
    micro, rows, _ = q.shape
    keys = kv.shape[1]
    q_spec, k_spec, v_spec, qs_spec, ks_spec, gain_spec = attention_specs(rows, keys)
    return pl.pallas_call(
        forward_kernel,
        grid=(micro, N_PAIRS),
        in_specs=[q_spec, k_spec, v_spec, qs_spec, ks_spec, gain_spec, gain_spec],
        out_specs=q_spec,
        out_shape=jax.ShapeDtypeStruct((micro, rows, QUERY_COLUMNS), BF),
        cost_estimate=attention_cost(micro, rows, keys, 2),
        name="attend",
    )(q, kv, kv, q_seg, k_seg, gq, gk)


def attend_back(q, kv, grad_out, q_seg, k_seg, gq, gk):
    micro, rows, _ = q.shape
    keys = kv.shape[1]
    behind = keys - rows
    q_spec, k_spec, v_spec, qs_spec, ks_spec, gain_spec = attention_specs(rows, keys)
    own_spec = pl.BlockSpec((1, rows, PAIR), lambda s, p: (s, 0, p))
    halo_spec = pl.BlockSpec((1, behind, PAIR), lambda s, p: (s, 0, p))
    own = jax.ShapeDtypeStruct((micro, rows, KEY_COLUMNS), F32)
    halo = jax.ShapeDtypeStruct((micro, behind, KEY_COLUMNS), BF)
    return pl.pallas_call(
        backward_kernel,
        grid=(micro, N_PAIRS),
        in_specs=[q_spec, k_spec, v_spec, q_spec, qs_spec, ks_spec, gain_spec, gain_spec],
        out_specs=[q_spec, own_spec, own_spec, halo_spec, halo_spec, pl.BlockSpec((8, PAIR), lambda s, p: (0, 0))],
        out_shape=[
            jax.ShapeDtypeStruct((micro, rows, QUERY_COLUMNS), BF),
            own, own, halo, halo,
            jax.ShapeDtypeStruct((8, PAIR), F32),
        ],
        cost_estimate=attention_cost(micro, rows, keys, 5),
        name="attend_back",
    )(q, kv, kv, grad_out, q_seg, k_seg, gq, gk)


def fold_key_values(gk_own, gv_own, others, kv_own, gk):
    micro, rows, _ = gk_own.shape
    half = pl.BlockSpec((1, rows, KEY_COLUMNS), lambda s: (s, 0, 0))
    full = pl.BlockSpec((1, rows, 2 * KEY_COLUMNS), lambda s: (s, 0, 0))
    return pl.pallas_call(
        functools.partial(fold_kernel, len(others)),
        grid=(micro,),
        in_specs=[half, half] + [full] * len(others) + [half, pl.BlockSpec((1, PAIR), lambda s: (0, 0))],
        out_specs=[full, pl.BlockSpec((1, 1, PAIR), lambda s: (s, 0, 0))],
        out_shape=[
            jax.ShapeDtypeStruct((micro, rows, 2 * KEY_COLUMNS), BF),
            jax.ShapeDtypeStruct((micro, 1, PAIR), F32),
        ],
        name="fold_key_values",
    )(gk_own, gv_own, *others, kv_own, gk)


def far_blocks(block):
    size, me = lax.axis_size("far"), lax.axis_index("far")
    if size > 4:
        return lax.all_gather(block, "far", axis=0, tiled=False)
    found = [block]
    for distance in range(1, size):
        found.append(lax.ppermute(block, "far", [(i, (i + distance) % size) for i in range(size)]))
    ordered = []
    for at in range(size):
        offset = (me - at) % size
        chosen = found[0]
        for distance in range(1, size):
            chosen = jnp.where(offset == distance, found[distance], chosen)
        ordered.append(chosen)
    return jnp.stack(ordered)


def far_sum(blocks):
    size, me = lax.axis_size("far"), lax.axis_index("far")
    if size > 4:
        return lax.psum_scatter(blocks, "far", scatter_dimension=0, tiled=True)[0].astype(F32)
    found = [pick(blocks, me, 0)]
    for distance in range(1, size):
        leaving = pick(blocks, (me + distance) % size, 0)
        found.append(lax.ppermute(leaving, "far", [(i, (i + distance) % size) for i in range(size)]))
    total = found[0].astype(F32)
    for other in found[1:]:
        total = total + other.astype(F32)
    return total


def exchange_sum(blocks, axis, index, at):
    other = swap(pick(blocks, 1 - index, at).astype(BF), axis)
    return (pick(blocks, index, at).astype(F32) + other.astype(F32)).astype(BF)


def exchange(block, axis, index):
    return in_order(block, swap(block, axis), index)


def gather_all(shard, index):
    n, k, w = index
    half, width = shard.shape
    part = far_blocks(shard.astype(BF).T)
    cut = width // 2
    one = exchange(exchange(part[:, :cut], "near", n), "wsh", w)
    two = exchange(exchange(part[:, cut:], "wsh", w), "near", n)
    one = exchange(one, "core", k).transpose(1, 3, 2, 0, 4, 5)
    two = exchange(two, "core", k).transpose(2, 3, 1, 0, 4, 5)
    both = jnp.concatenate([one, two], axis=4)
    return both.reshape(2, -1, half)


def scatter_all(halves, index):
    n, k, w = index
    columns, half = halves[0].shape
    far = lax.axis_size("far")
    width = columns // (4 * far)
    blocks = jnp.stack(halves).astype(BF).reshape(2, far, 2, 2, width, half)
    part = exchange_sum(blocks, "core", k, 3)
    cut = width // 2
    one = exchange_sum(exchange_sum(part[:, :, :, :cut], "near", n, 2), "wsh", w, 0)
    two = exchange_sum(exchange_sum(part[:, :, :, cut:], "wsh", w, 0), "near", n, 1)
    return far_sum(jnp.concatenate([one, two], axis=1)).T


def gather_blk(block):
    return lax.all_gather(block, BLK, axis=0, tiled=False)


def upgate_quarter(shard, w):
    rows, width = shard.shape
    halves = shard.astype(BF).T.reshape(2, width // 2, rows)
    other = swap(pick(halves, 1 - w, 0), "wsh")
    mine = pick(halves, w, 0)
    both = jnp.where(w == 0, jnp.concatenate([mine, other], 1), jnp.concatenate([other, mine], 1))
    return both


def upgate_shard(part, w):
    units, rows = part.shape
    halves = part.astype(BF).reshape(units, 2, rows // 2)
    other = swap(pick(halves, 1 - w, 1), "wsh")
    both = in_order(pick(halves, w, 1), other, w)
    return both.reshape(2 * units, rows // 2).T.astype(F32)


def down_quarter(shard, units, k, w):
    rows, width = shard.shape
    count = rows // (4 * units)
    parts = shard.astype(BF).T.reshape(width, count, 2, 2, units)
    other = swap(pick(parts, 1 - w, 3), "wsh")
    both = in_order(pick(parts, w, 3), other, w)
    other = swap(pick(both, 1 - k, 3), "core")
    both = in_order(pick(both, k, 3), other, k)
    return both.transpose(0, 2, 1, 3, 4).reshape(2 * width, 2 * count * units)


def down_shard(part, units, k, w):
    width, total = part.shape[0] // 2, part.shape[1]
    count = total // (2 * units)
    parts = part.astype(BF).reshape(2, width, 2, count, units)
    other = swap(pick(parts, 1 - k, 0), "core")
    both = in_order(pick(parts, k, 0), other, k)
    other = swap(pick(both, 1 - w, 2), "wsh")
    both = in_order(pick(both, w, 2), other, w)
    return both.transpose(3, 1, 0, 4, 2).reshape(4 * count * units, width).astype(F32)


def four_tokens(block):
    across = swap(block, "wsh")
    return jnp.concatenate([block, swap(block, "core"), across, swap(across, "core")])


def four_sum(partial):
    rows = partial.shape[0] // 4
    leaving = jnp.concatenate([partial[3 * rows :], partial[rows : 2 * rows]]).astype(BF)
    other = swap(leaving, "core").astype(F32)
    across = swap((partial[2 * rows : 3 * rows] + other[:rows]).astype(BF), "wsh")
    return partial[:rows] + other[rows:] + across.astype(F32)


def finish_kernel(early_ref, late_ref, m_ref, mean_ref, sq_ref, g_out, w_out, f_out, s_out, n_out, r_out):
    row = lax.broadcasted_iota(jnp.int32, (17, 128), 0)
    lane = lax.broadcasted_iota(jnp.int32, (17, 128), 1)
    grad = jnp.concatenate([late_ref[0:8, :], early_ref[0:8, :], late_ref[9:10, :]], axis=0)
    first, second, update = lamb_moments(grad, mean_ref[...], sq_ref[...])
    g_out[...] = grad
    f_out[...] = first
    s_out[...] = second
    master = m_ref[...]
    squares = early_ref[8:9, :] + late_ref[8:9, :]
    at = lax.broadcasted_iota(jnp.int32, (1, 128), 1)
    segment = jnp.where(row < 8, 0, jnp.where(row < 16, 1, jnp.where(lane < HEAD_WIDTH, 2, 3)))
    spot_row = lax.broadcasted_iota(jnp.int32, (2, 8), 0)
    spot_col = lax.broadcasted_iota(jnp.int32, (2, 8), 1)
    norms = jnp.zeros((2, 8), F32)
    ratio_lane = jnp.zeros((1, 128), F32)
    ratio_gain = jnp.zeros((17, 128), F32)
    for i in range(8):
        if i < 4:
            weight_sq = jnp.sum(jnp.where(at == i, squares, 0.0), keepdims=True)
            update_sq = jnp.sum(jnp.where(at == 4 + i, squares, 0.0), keepdims=True)
        else:
            weight_sq = jnp.sum(jnp.where(segment == i - 4, master * master, 0.0), keepdims=True)
            update_sq = jnp.sum(jnp.where(segment == i - 4, update * update, 0.0), keepdims=True)
        weight_norm, update_norm = jnp.sqrt(weight_sq), jnp.sqrt(update_sq)
        ratio = weight_norm / (update_norm + EPS_ADAM)
        norms = jnp.where(spot_col == i, jnp.where(spot_row == 0, weight_norm, update_norm), norms)
        if i < 4:
            ratio_lane = jnp.where(at == i, ratio, ratio_lane)
        else:
            ratio_gain = jnp.where(segment == i - 4, ratio, ratio_gain)
    n_out[...] = norms
    r_out[...] = ratio_lane
    w_out[...] = master - RATE * ratio_gain * update


def finish(early, late, master, mean, square):
    shaped = [v.reshape(17, 128) for v in (master, mean, square)]
    plane = jax.ShapeDtypeStruct((17, 128), F32)
    *gains, norms, ratios = pl.pallas_call(
        finish_kernel,
        out_shape=[plane] * 4 + [jax.ShapeDtypeStruct((2, 8), F32), jax.ShapeDtypeStruct((1, 128), F32)],
        name="finish",
    )(early, late, *shaped)
    return [g.reshape(GAINS) for g in gains], norms, ratios[0]


def in_lanes(values):
    lane = lax.broadcasted_iota(jnp.int32, (1, 128), 1)
    row = jnp.zeros((1, 128), F32)
    for at, value in values:
        row = jnp.where(lane == at, value, row)
    return row


def local(
    tokens, segment_ids, cotangent,
    qkv_master, qkv_mean, qkv_square,
    proj_master, proj_mean, proj_square,
    upgate_master, upgate_mean, upgate_square,
    down_master, down_mean, down_square,
    gain_master, gain_mean, gain_square,
):
    micro, extent, _ = tokens.shape
    rows = micro * extent
    n_ctx, far = lax.axis_size(CTX), lax.axis_size("far")
    depth = n_ctx // 4
    here, n, k, w = (lax.axis_index(a) for a in (CTX, "near", "core", "wsh"))
    index = (n, k, w)
    units = upgate_master.shape[1] // 2
    half = D // 2
    attn_gain = gain_master[:D]
    ffn_gain = gain_master[D : 2 * D]
    query_gain = gain_master[2 * D : 2 * D + HEAD_WIDTH]
    key_gain = gain_master[2 * D + HEAD_WIDTH :]
    gq = jnp.tile(query_gain, 2)[None]
    gk = jnp.tile(key_gain, 2)[None]

    qkv_t = gather_all(qkv_master, index)
    proj_t = gather_all(proj_master, index)
    upgate_t = gather_blk(upgate_quarter(upgate_master, w)).reshape(2, -1, D)
    gate_t, up_t = upgate_t[0], upgate_t[1]
    down_t = gather_blk(down_quarter(down_master, units, k, w)).reshape(D, -1)

    extra = jnp.pad(segment_ids.astype(BF).reshape(1, rows), ((0, 15), (0, D - rows)))
    package = jnp.concatenate([tokens.reshape(rows, D), extra])
    blocks, segs = [tokens], [segment_ids]
    for distance in range(1, depth + 1):
        came = from_earlier(package, distance)
        blocks.insert(0, came[:rows].reshape(micro, extent, D))
        seg = came[rows, :rows].reshape(micro, extent).astype(jnp.int32)
        segs.insert(0, jnp.where(here >= distance, seg, -1))
    keys = (depth + 1) * extent
    around = jnp.concatenate(blocks, axis=1).astype(F32)
    k_seg = jnp.concatenate(segs, axis=1)[:, None, :]
    q_seg = segment_ids[:, :, None]
    normed_around = rms_norm(around, attn_gain)[0].astype(BF).reshape(micro * keys, D)
    inputs = tokens.astype(F32).reshape(rows, D)
    normed, inv_one = rms_norm(inputs, attn_gain)
    normed_low = normed.astype(BF)
    q_raw = dot_nt(normed_low[:, :half], qkv_t[0, :QUERY_COLUMNS])
    q_raw = q_raw + dot_nt(normed_low[:, half:], qkv_t[1, :QUERY_COLUMNS])
    q_raw = q_raw.reshape(micro, extent, QUERY_COLUMNS)
    kv_raw = dot_nt(normed_around[:, :half], qkv_t[0, QUERY_COLUMNS:])
    kv_raw = kv_raw + dot_nt(normed_around[:, half:], qkv_t[1, QUERY_COLUMNS:])
    kv_raw = kv_raw.reshape(micro, keys, 2 * KEY_COLUMNS)
    attn_low = attend(q_raw, kv_raw, q_seg, k_seg, gq, gk).reshape(rows, QUERY_COLUMNS)

    cot_low = cotangent.reshape(rows, D)
    cot_four = four_tokens(cot_low)
    middle = inputs + dot_nt(attn_low[:, :half], proj_t[0]) + dot_nt(attn_low[:, half:], proj_t[1])
    normed_two, inv_two = rms_norm(middle, ffn_gain)
    two_four = four_tokens(normed_two.astype(BF))
    gate = dot_nt(two_four, gate_t)
    upper = dot_nt(two_four, up_t)
    grad_hidden = dot_nn(cot_four, down_t)
    sigmoid_gate = jax.nn.sigmoid(gate)
    activated = gate * sigmoid_gate
    hidden_low = (activated * upper).astype(BF)
    grad_gate = (grad_hidden * upper * sigmoid_gate * (1.0 + gate * (1.0 - sigmoid_gate))).astype(BF)
    grad_upper = (grad_hidden * activated).astype(BF)
    grad_two = four_sum(dot_nn(grad_gate, gate_t) + dot_nn(grad_upper, up_t))
    gate_part = dot_tn(grad_gate, two_four).astype(BF).reshape(far // 2, 2, units, D)
    up_part = dot_tn(grad_upper, two_four).astype(BF).reshape(far // 2, 2, units, D)
    down_part = dot_tn(cot_four, hidden_low).astype(BF).reshape(far, 2, -1, hidden_low.shape[1])
    gate_part = exchange_sum(gate_part, "near", n, 1)
    up_part = exchange_sum(up_part, "near", n, 1)
    upgate_part = far_sum(jnp.concatenate([gate_part, up_part]))
    down_part = far_sum(exchange_sum(down_part, "near", n, 1))
    block_out = (middle + four_sum(dot_nt(hidden_low, down_t))).astype(BF).reshape(tokens.shape)

    grad_middle, ffn_rows = norm_back(middle, inv_two, ffn_gain, grad_two)
    grad_middle = grad_middle + cot_low.astype(F32)
    grad_middle_low = grad_middle.astype(BF)
    proj_halves = [dot_tn(grad_middle_low, attn_low[:, :half]), dot_tn(grad_middle_low, attn_low[:, half:])]
    proj_grad = scatter_all(proj_halves, index)
    grad_attn = jnp.concatenate([dot_nn(grad_middle_low, proj_t[i]) for i in range(2)], axis=1)
    grad_attn = grad_attn.astype(BF).reshape(micro, extent, QUERY_COLUMNS)
    grad_q, gk_own, gv_own, gk_halo, gv_halo, query_rows = attend_back(
        q_raw, kv_raw, grad_attn, q_seg, k_seg, gq, gk
    )
    halo = jnp.concatenate([gk_halo, gv_halo], axis=2).reshape(micro, depth, extent, 2 * KEY_COLUMNS)
    others = [to_earlier(halo[:, depth - distance], distance) for distance in range(1, depth + 1)]
    grad_kv, key_rows = fold_key_values(gk_own, gv_own, others, kv_raw[:, keys - extent :], gk)
    grad_projected = jnp.concatenate(
        [grad_q.reshape(rows, QUERY_COLUMNS), grad_kv.reshape(rows, 2 * KEY_COLUMNS)], axis=1
    )
    qkv_halves = [dot_tn(grad_projected, normed_low[:, :half]), dot_tn(grad_projected, normed_low[:, half:])]
    qkv_grad = scatter_all(qkv_halves, index)
    grad_normed = jnp.concatenate([dot_nn(grad_projected, qkv_t[i]) for i in range(2)], axis=1)
    grad_in, attn_rows = norm_back(inputs, inv_one, attn_gain, grad_normed)
    input_grad = (grad_middle + grad_in).reshape(tokens.shape)
    upgate_grad = upgate_shard(upgate_part, w)
    down_grad = down_shard(down_part, units, k, w)

    masters = (qkv_master, proj_master, upgate_master, down_master)
    grads = (qkv_grad, proj_grad, upgate_grad, down_grad)
    means = (qkv_mean, proj_mean, upgate_mean, down_mean)
    squares = (qkv_square, proj_square, upgate_square, down_square)
    firsts, seconds, updates = [], [], []
    for master, grad, mean, square in zip(masters, grads, means, squares):
        first, second, direction = lamb_moments(grad, mean, square)
        firsts.append(first)
        seconds.append(second)
        updates.append(direction + DECAY * master)
    master_sq = [(i, jnp.sum(masters[i] * masters[i])) for i in range(4)]
    update_sq = [(4 + i, jnp.sum(updates[i] * updates[i])) for i in range(4)]
    query_row = query_rows[0:1]
    key_row = jnp.sum(key_rows, axis=0)
    heads_row = jnp.concatenate(
        [query_row[:, :HEAD_WIDTH] + query_row[:, HEAD_WIDTH:], key_row[:, :HEAD_WIDTH] + key_row[:, HEAD_WIDTH:]], axis=1
    )
    early = jnp.concatenate([jnp.sum(ffn_rows, axis=0).reshape(8, 128), in_lanes(master_sq + update_sq[1:])])
    late = jnp.concatenate([jnp.sum(attn_rows, axis=0).reshape(8, 128), in_lanes(update_sq[:1]), heads_row])
    early, late = total_everywhere(early), total_everywhere(late)
    gain_outs, lamb_norms, ratios = finish(early, late, gain_master, gain_mean, gain_square)
    gain_grad, gain_weight, gain_first, gain_second = gain_outs
    outs = [block_out, input_grad]
    for i in range(4):
        outs += [grads[i], masters[i] - RATE * ratios[i] * updates[i], firsts[i], seconds[i]]
    return (*outs, gain_grad, gain_weight, gain_first, gain_second, lamb_norms)


def solution(mesh):
    n_ctx, n_wsh = mesh.devices.shape
    fine = Mesh(mesh.devices.reshape(n_ctx // 4, 2, 2, n_wsh), EVERY)
    sequence = P("wsh", CTX)
    weight = P("wsh", CTX)
    return jax.shard_map(
        local,
        mesh=fine,
        in_specs=(sequence,) * 3 + (weight,) * 12 + (P(),) * 3,
        out_specs=(sequence,) * 2 + (weight,) * 16 + (P(),) * 5,
        check_vma=False,
    )
```

```python
import functools

import jax
import jax.numpy as jnp
from jax import lax
from jax.experimental import pallas as pl
from jax.experimental.pallas import tpu as pltpu
from jax.sharding import Mesh
from jax.sharding import PartitionSpec as P


D = 1024
QUERY_HEADS = 16
KEY_VALUE_HEADS = 8
HEAD_WIDTH = 64
STEP = 10
GAINS = 2176
QUERY_COLUMNS = QUERY_HEADS * HEAD_WIDTH
KEY_COLUMNS = KEY_VALUE_HEADS * HEAD_WIDTH
PAIR = 2 * HEAD_WIDTH
N_PAIRS = KEY_VALUE_HEADS // 2

EPS_NORM = 1e-05
BETA_ONE = 0.9
BETA_TWO = 0.999
EPS_ADAM = 1e-06
DECAY = 0.01
RATE = 0.5
NEGATIVE_FILLER = -1e30

FAR = ("hi", "top", "low")
CTX = (*FAR, "near", "core")
QUARTERS = ("hi", "top")
EVERY = (*CTX, "wsh")
OTHERS = ("hi", "wsh", "low", "near")

BF = jnp.bfloat16
F32 = jnp.float32


def swap(block, axis):
    return lax.ppermute(block, axis, [(0, 1), (1, 0)])


def from_earlier(package, depth):
    here, quarter, n, k = (lax.axis_index(a) for a in (CTX, QUARTERS, "near", "core"))
    if lax.axis_size("low") > 1:
        size = lax.axis_size(CTX)
        blocks, exists = [], []
        for distance in range(1, depth + 1):
            route = [(i - distance, i) for i in range(distance, size)]
            blocks.append(lax.ppermute(package, CTX, route))
            exists.append(here >= distance)
        return blocks, exists
    before = lax.ppermute(package, QUARTERS, [(0, 1), (1, 2), (2, 3)])
    across = swap(jnp.where(n == 0, package, before), "near")
    beside = swap(jnp.where(k == 0, package, before), "core")
    diagonal = swap(across, "core")
    later = quarter > 0
    return [before, across, beside, diagonal], [later, later | (n == 1), later | (k == 1), later | (n == 1)]


def to_earlier(parts, own):
    n, k = lax.axis_index("near"), lax.axis_index("core")
    if lax.axis_size("low") > 1:
        size = lax.axis_size(CTX)
        for distance, part in enumerate(parts, 1):
            route = [(i, i - distance) for i in range(distance, size)]
            own = own + lax.ppermute(part, CTX, route).astype(F32)
        return own
    before, across, beside, diagonal = parts
    beside = swap(beside, "core").astype(F32)
    diagonal = swap(diagonal, "core").astype(F32)
    across = swap((across.astype(F32) + diagonal).astype(BF), "near").astype(F32)
    before = before.astype(F32) + jnp.where(k == 1, beside, 0.0) + jnp.where(n == 1, across, 0.0)
    after = lax.ppermute(before.astype(BF), QUARTERS, [(1, 0), (2, 1), (3, 2)]).astype(F32)
    return own + jnp.where(k == 0, beside, 0.0) + jnp.where(n == 0, across, 0.0) + after


def in_order(mine, other, index, at=0):
    return jnp.where(index == 0, jnp.stack([mine, other], at), jnp.stack([other, mine], at))


def pick(array, index, axis):
    return lax.dynamic_index_in_dim(array, index, axis, keepdims=False)


def total_everywhere(block):
    for axis in ("core", "wsh", "near", "hi", "top", "low"):
        size = lax.axis_size(axis)
        step = 1
        while step < size:
            block = block + lax.ppermute(block, axis, [(i, i ^ step) for i in range(size)])
            step *= 2
    return block


def rms_norm(inputs, gain):
    inverse = lax.rsqrt(jnp.mean(inputs * inputs, axis=-1, keepdims=True) + EPS_NORM)
    return inputs * inverse * gain, inverse


def norm_back(inputs, inverse, gain, grad_out):
    weighted = grad_out * gain
    inner = jnp.mean(weighted * inputs, axis=-1, keepdims=True)
    grad_in = inverse * weighted - inputs * (inverse * inverse * inverse) * inner
    return grad_in, grad_out * inputs * inverse


def lamb_moments(grad, mean, square):
    first = BETA_ONE * mean + (1.0 - BETA_ONE) * grad
    second = BETA_TWO * square + (1.0 - BETA_TWO) * grad * grad
    bias_one = 1.0 - BETA_ONE**STEP
    bias_two = 1.0 - BETA_TWO**STEP
    direction = first / bias_one / (jnp.sqrt(second / bias_two) + EPS_ADAM)
    return first, second, direction


def low_half():
    return lax.broadcasted_iota(jnp.int32, (1, PAIR), 1) < HEAD_WIDTH


def dot_nt(a, b):
    return lax.dot_general(a, b, (((1,), (1,)), ((), ())), preferred_element_type=F32)


def dot_tn(a, b):
    return lax.dot_general(a, b, (((0,), (0,)), ((), ())), preferred_element_type=F32)


def dot_nn(a, b):
    return lax.dot_general(a, b, (((1,), (0,)), ((), ())), preferred_element_type=F32)


def half_sums(block):
    row = lax.broadcasted_iota(jnp.int32, (PAIR, PAIR), 0) < HEAD_WIDTH
    col = lax.broadcasted_iota(jnp.int32, (PAIR, PAIR), 1) < HEAD_WIDTH
    ones = jnp.where(row == col, 1.0, 0.0).astype(BF)
    high = block.astype(BF)
    rest = (block - high.astype(F32)).astype(BF)
    return dot_nn(high, ones) + dot_nn(rest, ones)


def head_norm(block, gain):
    inverse = lax.rsqrt(half_sums(block * block) * (1.0 / HEAD_WIDTH) + EPS_NORM)
    return block * inverse * gain, inverse


def head_norm_back(raw, inverse, gain, grad):
    weighted = grad * gain
    inner = half_sums(weighted * raw) * (1.0 / HEAD_WIDTH)
    return inverse * weighted - raw * (inverse * inverse * inverse) * inner


def spread(block):
    low = low_half()
    turned = pltpu.roll(block, HEAD_WIDTH, 1)
    return jnp.where(low, block, turned).astype(BF), jnp.where(low, turned, block).astype(BF)


def stacked(block):
    low = low_half()
    return jnp.concatenate([jnp.where(low, block, 0.0), jnp.where(low, 0.0, block)], axis=0).astype(BF)


def unstacked(block):
    rows = block.shape[0] // 2
    return jnp.where(low_half(), block[:rows], block[rows:])


def allowed_mask(q_seg, k_seg):
    rows = q_seg.shape[1]
    behind = (k_seg.shape[0] - 1) * rows
    columns = [jnp.broadcast_to(k_seg[i : i + 1], (rows, rows)).T for i in range(k_seg.shape[0])]
    k_column = jnp.concatenate(columns, axis=0)
    key = lax.broadcasted_iota(jnp.int32, k_column.shape, 0)
    query = lax.broadcasted_iota(jnp.int32, k_column.shape, 1)
    mask = (k_column == q_seg) & (key <= query + behind)
    return jnp.concatenate([mask, mask], axis=1)


def joined(ref):
    return ref[:, 0].reshape(-1, ref.shape[3])


def softmax_parts(scores, mask):
    filled = jnp.where(mask, scores, NEGATIVE_FILLER)
    top = jnp.max(filled, axis=0, keepdims=True)
    weights = jnp.exp(filled - top)
    return weights, 1.0 / jnp.sum(weights, axis=0, keepdims=True)


def forward_kernel(q_ref, k_ref, v_ref, qs_ref, ks_ref, gq_ref, gk_ref, o_ref):
    mask = allowed_mask(qs_ref[0], ks_ref[0])
    key_pair = spread(head_norm(joined(k_ref), gk_ref[...])[0])
    value_pair = spread(joined(v_ref))
    for head in range(2):
        at = pl.ds(head * PAIR, PAIR)
        query = head_norm(q_ref[0, :, at], gq_ref[...])[0].astype(BF).astype(F32)
        scores = dot_nt(key_pair[head], stacked(query * HEAD_WIDTH**-0.5))
        weights, inverse = softmax_parts(scores, mask)
        attended = dot_tn(value_pair[head], weights.astype(BF)) * inverse
        o_ref[0, :, at] = unstacked(attended.T).astype(BF)


def backward_kernel(
    q_ref, k_ref, v_ref, go_ref, qs_ref, ks_ref, gq_ref, gk_ref, gq_out, gk_out, gv_out, gain_out
):
    mask = allowed_mask(qs_ref[0], ks_ref[0])
    raw_key = joined(k_ref)
    normed_key, inverse_key = head_norm(raw_key, gk_ref[...])
    key_pair = spread(normed_key)
    value_pair = spread(joined(v_ref))
    low = low_half()
    shape = (k_ref.shape[0], *k_ref.shape[2:])

    @pl.when((pl.program_id(0) == 0) & (pl.program_id(1) == 0))
    def _():
        gain_out[...] = jnp.zeros_like(gain_out)

    grad_keys, grad_values = [], []
    for head in range(2):
        at = pl.ds(head * PAIR, PAIR)
        raw = q_ref[0, :, at]
        normed, inverse_norm = head_norm(raw, gq_ref[...])
        query = stacked(normed.astype(BF).astype(F32) * HEAD_WIDTH**-0.5)
        weights, inverse = softmax_parts(dot_nt(key_pair[head], query), mask)
        probs = weights * inverse
        grad_out = stacked(go_ref[0, :, at].astype(F32))
        grad_probs = dot_nt(value_pair[head], grad_out)
        delta = jnp.sum(probs * grad_probs, axis=0, keepdims=True)
        grad_scores = (probs * (grad_probs - delta)).astype(BF)
        grad_query = unstacked(dot_tn(key_pair[head], grad_scores).T) * HEAD_WIDTH**-0.5
        key_part = dot_nn(grad_scores, query)
        value_part = dot_nn(probs.astype(BF), grad_out)
        grad_keys.append(key_part + pltpu.roll(key_part, HEAD_WIDTH, 1))
        grad_values.append(value_part + pltpu.roll(value_part, HEAD_WIDTH, 1))
        gq_out[0, :, at] = head_norm_back(raw, inverse_norm, gq_ref[...], grad_query).astype(BF)
        gain_out[0:1, :] += jnp.sum(grad_query * raw * inverse_norm, axis=0, keepdims=True)
    grad_key = jnp.where(low, grad_keys[0], grad_keys[1])
    gain_out[1:2, :] += jnp.sum(grad_key * raw_key * inverse_key, axis=0, keepdims=True)
    gk_out[:, 0] = head_norm_back(raw_key, inverse_key, gk_ref[...], grad_key).astype(BF).reshape(shape)
    gv_out[:, 0] = jnp.where(low, grad_values[0], grad_values[1]).astype(BF).reshape(shape)


def attention_specs(rows, count):
    q_spec = pl.BlockSpec((1, rows, 2 * PAIR), lambda s, p: (s, 0, p))
    k_spec = pl.BlockSpec((count, 1, rows, PAIR), lambda s, p: (0, s, 0, p))
    v_spec = pl.BlockSpec((count, 1, rows, PAIR), lambda s, p: (0, s, 0, N_PAIRS + p))
    qs_spec = pl.BlockSpec((1, 1, rows), lambda s, p: (s, 0, 0))
    ks_spec = pl.BlockSpec((1, count, rows), lambda s, p: (s, 0, 0))
    gain_spec = pl.BlockSpec((1, PAIR), lambda s, p: (0, 0))
    return q_spec, k_spec, v_spec, qs_spec, ks_spec, gain_spec


def attention_cost(micro, rows, keys, products):
    work = micro * QUERY_HEADS * rows * keys
    return pl.CostEstimate(
        flops=2 * 4 * PAIR * products * work,
        bytes_accessed=micro * (rows * 6 * QUERY_COLUMNS + keys * 8 * KEY_COLUMNS),
        transcendentals=work,
    )


def attend(q, kv, q_seg, k_seg, gq, gk):
    count, micro, rows, _ = kv.shape
    q_spec, k_spec, v_spec, qs_spec, ks_spec, gain_spec = attention_specs(rows, count)
    return pl.pallas_call(
        forward_kernel,
        grid=(micro, N_PAIRS),
        in_specs=[q_spec, k_spec, v_spec, qs_spec, ks_spec, gain_spec, gain_spec],
        out_specs=q_spec,
        out_shape=jax.ShapeDtypeStruct((micro, rows, QUERY_COLUMNS), BF),
        cost_estimate=attention_cost(micro, rows, count * rows, 2),
        name="attend",
    )(q, kv, kv, q_seg, k_seg, gq, gk)


def attend_back(q, kv, grad_out, q_seg, k_seg, gq, gk):
    count, micro, rows, _ = kv.shape
    q_spec, k_spec, v_spec, qs_spec, ks_spec, gain_spec = attention_specs(rows, count)
    part = jax.ShapeDtypeStruct((count, micro, rows, KEY_COLUMNS), BF)
    return pl.pallas_call(
        backward_kernel,
        grid=(micro, N_PAIRS),
        in_specs=[q_spec, k_spec, v_spec, q_spec, qs_spec, ks_spec, gain_spec, gain_spec],
        out_specs=[q_spec, k_spec, k_spec, pl.BlockSpec((8, PAIR), lambda s, p: (0, 0))],
        out_shape=[
            jax.ShapeDtypeStruct((micro, rows, QUERY_COLUMNS), BF),
            part,
            part,
            jax.ShapeDtypeStruct((8, PAIR), F32),
        ],
        cost_estimate=attention_cost(micro, rows, count * rows, 5),
        name="attend_back",
    )(q, kv, kv, grad_out, q_seg, k_seg, gq, gk)


def far_blocks(block):
    size, me = lax.axis_size(FAR), lax.axis_index(FAR)
    if size > 4:
        return lax.all_gather(block, FAR, axis=0, tiled=False)
    found = [block]
    for distance in range(1, size):
        found.append(lax.ppermute(block, FAR, [(i, (i + distance) % size) for i in range(size)]))
    ordered = []
    for at in range(size):
        offset = (me - at) % size
        chosen = found[0]
        for distance in range(1, size):
            chosen = jnp.where(offset == distance, found[distance], chosen)
        ordered.append(chosen)
    return jnp.stack(ordered)


def far_parts(blocks):
    size, me = lax.axis_size(FAR), lax.axis_index(FAR)
    if size > 4:
        return [lax.psum_scatter(blocks, FAR, scatter_dimension=0, tiled=True)[0]]
    found = [pick(blocks, me, 0)]
    for distance in range(1, size):
        leaving = pick(blocks, (me + distance) % size, 0)
        found.append(lax.ppermute(leaving, FAR, [(i, (i + distance) % size) for i in range(size)]))
    return found


def exchange_sum(blocks, axis, index, at):
    other = swap(pick(blocks, 1 - index, at), axis)
    return (pick(blocks, index, at).astype(F32) + other.astype(F32)).astype(BF)


def lane_half(block, index):
    half = block.shape[-1] // 2
    return jnp.where(index == 0, block[..., :half], block[..., half:])


def exchange_lanes_sum(blocks, index):
    other = swap(lane_half(blocks, 1 - index), "wsh")
    return (lane_half(blocks, index).astype(F32) + other.astype(F32)).astype(BF)


def exchange(block, axis, index, at):
    return in_order(block, swap(block, axis), index, at)


def interleave_kernel(k_ref, mine_ref, other_ref, *outs):
    is_mine = pl.program_id(0) == k_ref[0]
    start = 0
    for out in outs:
        at = pl.ds(start, out.shape[2])
        start += out.shape[2]

        @pl.when(is_mine)
        def _(out=out, at=at):
            out[0, 0] = mine_ref[0, at, :]

        @pl.when(jnp.logical_not(is_mine))
        def _(out=out, at=at):
            out[0, 0] = other_ref[0, at, :]


def interleave(mine, other, k, widths):
    columns = mine.shape[-1]
    mine, other = (v.reshape(-1, sum(widths), columns) for v in (mine, other))
    count = mine.shape[0]

    def block_of(core):
        def index(c, i, k_ref):
            wanted = k_ref[0] if core == 0 else 1 - k_ref[0]
            return jnp.where(c == wanted, i, jnp.where(c < wanted, 0, count - 1)), 0, 0

        return pl.BlockSpec((1, sum(widths), columns), index)

    outs = pl.pallas_call(
        interleave_kernel,
        grid_spec=pltpu.PrefetchScalarGridSpec(
            num_scalar_prefetch=1,
            grid=(2, count),
            in_specs=[block_of(0), block_of(1)],
            out_specs=[pl.BlockSpec((1, 1, width, columns), lambda c, i, _: (i, c, 0, 0)) for width in widths],
        ),
        out_shape=[jax.ShapeDtypeStruct((count, 2, width, columns), BF) for width in widths],
        cost_estimate=pl.CostEstimate(flops=0, bytes_accessed=8 * mine.size, transcendentals=0),
        name="interleave",
    )(k.reshape(1).astype(jnp.int32), mine, other)
    return [v.reshape(-1, columns) for v in outs]


def gather_all(shards, index):
    n, k, w = index
    widths = [shard.shape[1] for shard in shards]
    part = far_blocks(jnp.concatenate([shard.astype(BF).T for shard in shards]))
    cut = part.shape[0] // 2
    one = exchange(part[:cut], "near", n, 1)
    two = exchange_lanes(part[cut:], w)
    one = exchange_lanes(one, w)
    two = exchange(two, "near", n, 1)
    firsts = interleave(one, swap(one, "core"), k, widths)
    seconds = interleave(two, swap(two, "core"), k, widths)
    return [half for pair in zip(firsts, seconds) for half in pair]


def grad_kernel(firsts, k_ref, *refs):
    groups = len(firsts) - 1
    keep, leave = refs[2 * groups :]
    width = keep.shape[1]
    for i in range(groups):

        @pl.when((pl.program_id(0) >= firsts[i]) & (pl.program_id(0) < firsts[i + 1]))
        def _(i=i):
            whole = dot_tn(refs[2 * i][...], refs[2 * i + 1][...])
            is_first = k_ref[0] == 0
            keep[0] = jnp.where(is_first, whole[:width], whole[width:]).astype(BF)
            leave[0] = jnp.where(is_first, whole[width:], whole[:width]).astype(BF)


def weight_grad(pairs, k):
    chips = lax.axis_size(FAR) * lax.axis_size("near")
    chip_width = sum(a.shape[1] for a, _ in pairs) // chips
    if chip_width % 128:
        whole = jnp.concatenate([dot_tn(a, b).astype(BF) for a, b in pairs])
        whole = whole.reshape(chips, 2, chip_width // 2, -1)
        return pick(whole, k, 1), pick(whole, 1 - k, 1)
    firsts, specs, operands = [0], [], []
    for a, b in pairs:
        start, count = firsts[-1], a.shape[1] // chip_width
        block = pl.BlockSpec(
            (a.shape[0], chip_width), lambda i, _, s=start, c=count: (0, jnp.clip(i - s, 0, c - 1))
        )
        specs += [block, pl.BlockSpec(b.shape, lambda i, _: (0, 0))]
        operands += [a, b]
        firsts.append(start + count)
    columns = pairs[0][1].shape[1]
    out = pl.BlockSpec((1, chip_width // 2, columns), lambda i, _: (i, 0, 0))
    shape = jax.ShapeDtypeStruct((chips, chip_width // 2, columns), BF)
    flops = sum(2 * a.shape[0] * a.shape[1] * columns for a, _ in pairs)
    return pl.pallas_call(
        functools.partial(grad_kernel, tuple(firsts)),
        grid_spec=pltpu.PrefetchScalarGridSpec(
            num_scalar_prefetch=1, grid=(chips,), in_specs=specs, out_specs=[out, out]
        ),
        out_shape=[shape, shape],
        cost_estimate=pl.CostEstimate(
            flops=flops, bytes_accessed=2 * sum(a.size + b.size for a, b in pairs) + 4 * chips * chip_width * columns, transcendentals=0
        ),
        name="weight_grad",
    )(k.reshape(1).astype(jnp.int32), *operands)


def scatter_all(grads, index):
    n, _, w = index
    keep, leave = grads
    far = lax.axis_size(FAR)
    cut = far // 2
    part = (keep.astype(F32) + swap(leave, "core").astype(F32)).astype(BF)
    part = part.reshape(far, 2, *part.shape[1:])
    one = exchange_sum(part[:cut], "near", n, 1)
    two = exchange_lanes_sum(part[cut:], w)
    one = exchange_lanes_sum(one, w)
    two = exchange_sum(two, "near", n, 1)
    return far_parts(jnp.concatenate([one, two]))


def exchange_lanes(block, index):
    other = swap(block, "wsh")
    first = jnp.concatenate([block, other], axis=-1)
    return jnp.where(index == 0, first, jnp.concatenate([other, block], axis=-1))


def gather_upgate(shard):
    whole = lax.all_gather(shard.astype(BF).T, OTHERS, axis=0, tiled=False)
    whole = whole.reshape(2, 2, -1, shard.shape[0])
    return [jnp.concatenate([whole[i, 0], whole[i, 1]], axis=1) for i in range(2)]


def scatter_upgate(grad_gate, grad_upper, tokens):
    half = D // 2
    halves = (tokens[:, :half], tokens[:, half:])
    blocks = jnp.stack([dot_tn(a, b).astype(BF) for a in (grad_gate, grad_upper) for b in halves])
    blocks = blocks.reshape(2 * lax.axis_size(OTHERS) // 2, -1, half)
    return [lax.psum_scatter(blocks, OTHERS, scatter_dimension=0, tiled=True)[0]]


CROSS = ((0, 0), (1, 2), (2, 1), (3, 3))


def cross(block):
    return lax.ppermute(block, ("top", "wsh"), CROSS)


def gather_down(shard, k):
    rows, width = shard.shape
    low = lax.axis_size("low")
    parts = cross(shard.astype(BF).T).reshape(width, 2 * low, 2, rows // (4 * low))
    both = in_order(pick(parts, k, 2), swap(pick(parts, 1 - k, 2), "core"), k)
    both = both.reshape(2 * width, rows // 2)
    return lax.all_gather(both, OTHERS, axis=0, tiled=True)


def scatter_down(grad, k):
    total = grad.shape[1]
    low = lax.axis_size("low")
    blocks = grad.reshape(lax.axis_size(OTHERS), -1, total)
    part = lax.psum_scatter(blocks, OTHERS, scatter_dimension=0, tiled=True)[0]
    width = part.shape[0] // 2
    parts = part.reshape(2, width, 2 * low, total // (2 * low))
    both = in_order(pick(parts, k, 0), swap(pick(parts, 1 - k, 0), "core"), k)
    return [cross(both.transpose(1, 2, 0, 3).reshape(width, 2 * total))]


def four_tokens(block):
    across = swap(block, "top")
    return jnp.concatenate([block, swap(block, "core"), across, swap(across, "core")])


def four_sum(partial):
    rows = partial.shape[0] // 4
    leaving = jnp.concatenate([partial[3 * rows :], partial[rows : 2 * rows]]).astype(BF)
    other = swap(leaving, "core").astype(F32)
    across = swap((partial[2 * rows : 3 * rows] + other[:rows]).astype(BF), "top")
    return partial[:rows] + other[rows:] + across.astype(F32)


def finish_kernel(early_ref, late_ref, m_ref, mean_ref, sq_ref, g_out, w_out, f_out, s_out, n_out, r_out):
    row = lax.broadcasted_iota(jnp.int32, (17, 128), 0)
    lane = lax.broadcasted_iota(jnp.int32, (17, 128), 1)
    grad = jnp.concatenate([late_ref[0:8, :], early_ref[0:8, :], late_ref[9:10, :]], axis=0)
    first, second, update = lamb_moments(grad, mean_ref[...], sq_ref[...])
    g_out[...] = grad
    f_out[...] = first
    s_out[...] = second
    master = m_ref[...]
    squares = early_ref[8:9, :] + late_ref[8:9, :]
    at = lax.broadcasted_iota(jnp.int32, (1, 128), 1)
    segment = jnp.where(row < 8, 0, jnp.where(row < 16, 1, jnp.where(lane < HEAD_WIDTH, 2, 3)))
    spot_row = lax.broadcasted_iota(jnp.int32, (2, 8), 0)
    spot_col = lax.broadcasted_iota(jnp.int32, (2, 8), 1)
    norms = jnp.zeros((2, 8), F32)
    ratio_lane = jnp.zeros((1, 128), F32)
    ratio_gain = jnp.zeros((17, 128), F32)
    for i in range(8):
        if i < 4:
            weight_sq = jnp.sum(jnp.where(at == i, squares, 0.0), keepdims=True)
            update_sq = jnp.sum(jnp.where(at == 4 + i, squares, 0.0), keepdims=True)
        else:
            weight_sq = jnp.sum(jnp.where(segment == i - 4, master * master, 0.0), keepdims=True)
            update_sq = jnp.sum(jnp.where(segment == i - 4, update * update, 0.0), keepdims=True)
        weight_norm, update_norm = jnp.sqrt(weight_sq), jnp.sqrt(update_sq)
        ratio = weight_norm / (update_norm + EPS_ADAM)
        norms = jnp.where(spot_col == i, jnp.where(spot_row == 0, weight_norm, update_norm), norms)
        if i < 4:
            ratio_lane = jnp.where(at == i, ratio, ratio_lane)
        else:
            ratio_gain = jnp.where(segment == i - 4, ratio, ratio_gain)
    n_out[...] = norms
    r_out[...] = ratio_lane
    w_out[...] = master - RATE * ratio_gain * update


def finish(early, late, master, mean, square):
    shaped = [v.reshape(17, 128) for v in (master, mean, square)]
    plane = jax.ShapeDtypeStruct((17, 128), F32)
    *gains, norms, ratios = pl.pallas_call(
        finish_kernel,
        out_shape=[plane] * 4 + [jax.ShapeDtypeStruct((2, 8), F32), jax.ShapeDtypeStruct((1, 128), F32)],
        name="finish",
    )(early, late, *shaped)
    return [g.reshape(GAINS) for g in gains], norms, ratios[0]


def moments_kernel(which, steps, count, turn, *refs):
    parts = refs[:count]
    m_ref, s_ref, w_ref, g_out, f_out, s_out, u_out, sum_out, acc = refs[count:]
    step = pl.program_id(0)

    @pl.when(step == 0)
    def _():
        acc[...] = jnp.zeros_like(acc)

    grad = parts[0][...].astype(F32)
    for part in parts[1:]:
        grad += part[...].astype(F32)
    if turn:
        grad = grad.T
    master = w_ref[...]
    first, second, direction = lamb_moments(grad, m_ref[...], s_ref[...])
    update = direction + DECAY * master
    g_out[...] = grad
    f_out[...] = first
    s_out[...] = second
    u_out[...] = update
    acc[0:1, :] += jnp.sum(master * master, axis=0, keepdims=True)
    acc[1:2, :] += jnp.sum(update * update, axis=0, keepdims=True)

    @pl.when(step == steps - 1)
    def _():
        lane = lax.broadcasted_iota(jnp.int32, (1, 128), 1)
        master_sum = jnp.sum(acc[0:1, :], keepdims=True)
        update_sum = jnp.sum(acc[1:2, :], keepdims=True)
        sum_out[...] = jnp.where(lane == which, master_sum, jnp.where(lane == 4 + which, update_sum, 0.0))


def moments(which, parts, mean, square, master):
    rows, columns = master.shape
    turn = columns % 128 == 0
    steps = 4 if rows % 512 == 0 else 6
    if rows % (128 * steps):
        steps = 1
    tall = pl.BlockSpec((columns, rows // steps), lambda i: (0, i))
    block = pl.BlockSpec((rows // steps, columns), lambda i: (i, 0)) if turn else tall
    others = (mean, square, master) if turn else (mean.T, square.T, master.T)
    plane = jax.ShapeDtypeStruct(others[0].shape, F32)
    *outs, sums = pl.pallas_call(
        functools.partial(moments_kernel, which, steps, len(parts), turn),
        grid=(steps,),
        in_specs=[tall] * len(parts) + [block] * 3,
        out_specs=[block] * 4 + [pl.BlockSpec((1, 128), lambda i: (0, 0))],
        out_shape=[plane] * 4 + [jax.ShapeDtypeStruct((1, 128), F32)],
        scratch_shapes=[pltpu.VMEM((2, block.block_shape[1]), F32)],
        cost_estimate=pl.CostEstimate(
            flops=20 * rows * columns, bytes_accessed=32 * rows * columns, transcendentals=2 * rows * columns
        ),
        name="moments",
    )(*parts, *others)
    return *(outs if turn else [o.T for o in outs]), sums


def local(
    tokens, segment_ids, cotangent,
    qkv_master, qkv_mean, qkv_square,
    proj_master, proj_mean, proj_square,
    upgate_master, upgate_mean, upgate_square,
    down_master, down_mean, down_square,
    gain_master, gain_mean, gain_square,
):
    micro, extent, _ = tokens.shape
    rows = micro * extent
    n_ctx = lax.axis_size(CTX)
    depth = n_ctx // 4
    n, k, w = (lax.axis_index(a) for a in ("near", "core", "wsh"))
    index = (n, k, w)
    half = D // 2
    attn_gain = gain_master[:D]
    ffn_gain = gain_master[D : 2 * D]
    query_gain = gain_master[2 * D : 2 * D + HEAD_WIDTH]
    key_gain = gain_master[2 * D + HEAD_WIDTH :]
    gq = jnp.tile(query_gain, 2)[None]
    gk = jnp.tile(key_gain, 2)[None]

    extra = jnp.pad(segment_ids.astype(BF).reshape(1, rows), ((0, 15), (0, D - rows)))
    package = jnp.concatenate([tokens.reshape(rows, D), extra])
    halo, exists = from_earlier(package, depth)
    query_t, kv_t, *proj_t = gather_all((qkv_master, proj_master), index)
    gate_t, up_t = gather_upgate(upgate_master)
    down_t = gather_down(down_master, k)

    count = depth + 1
    around = jnp.concatenate([came[:rows] for came in halo] + [package[:rows]]).astype(F32)
    seg_rows = jnp.concatenate([came[rows : rows + 1, :rows] for came in halo] + [package[rows : rows + 1, :rows]])
    row = lax.broadcasted_iota(jnp.int32, (count, rows), 0)
    present = row == depth
    for i, there in enumerate(exists):
        present = present | ((row == i) & there)
    k_seg = jnp.where(present, seg_rows.astype(F32), -1.0).reshape(count, micro, extent).transpose(1, 0, 2)
    q_seg = segment_ids[:, None, :].astype(F32)
    normed_around = lax.optimization_barrier(rms_norm(around, attn_gain)[0].astype(BF))
    inputs = tokens.astype(F32).reshape(rows, D)
    inv_one = lax.rsqrt(jnp.mean(inputs * inputs, axis=-1, keepdims=True) + EPS_NORM)
    normed_low = normed_around[depth * rows :]
    q_raw = dot_nt(normed_low, query_t).reshape(micro, extent, QUERY_COLUMNS)
    kv_raw = dot_nt(normed_around, kv_t).reshape(count, micro, extent, 2 * KEY_COLUMNS)
    attn_low = attend(q_raw, kv_raw, q_seg, k_seg, gq, gk).reshape(rows, QUERY_COLUMNS)

    cot_low = cotangent.reshape(rows, D)
    cot_four = four_tokens(cot_low)
    middle = inputs + jnp.concatenate([dot_nt(attn_low, p) for p in proj_t], axis=1)
    normed_two, inv_two = rms_norm(middle, ffn_gain)
    two_four = four_tokens(normed_two.astype(BF))
    gate = dot_nt(two_four, gate_t)
    upper = dot_nt(two_four, up_t)
    grad_hidden = dot_nn(cot_four, down_t)
    sigmoid_gate = jax.nn.sigmoid(gate)
    activated = gate * sigmoid_gate
    hidden_low = (activated * upper).astype(BF)
    grad_gate = (grad_hidden * upper * sigmoid_gate * (1.0 + gate * (1.0 - sigmoid_gate))).astype(BF)
    grad_upper = (grad_hidden * activated).astype(BF)
    grad_two_part = dot_nn(grad_gate, gate_t) + dot_nn(grad_upper, up_t)
    grad_two = four_sum(grad_two_part)
    upgate_parts = scatter_upgate(grad_gate, grad_upper, two_four)
    down_parts = scatter_down(dot_tn(cot_four, hidden_low).astype(BF), k)
    block_out = (lax.optimization_barrier(middle) + four_sum(dot_nt(hidden_low, down_t))).astype(BF).reshape(tokens.shape)

    grad_middle, ffn_rows = norm_back(middle, inv_two, ffn_gain, grad_two)
    grad_middle = grad_middle + cot_low.astype(F32)
    grad_middle_low = grad_middle.astype(BF)
    proj_parts = scatter_all(weight_grad([(grad_middle_low, attn_low)], k), index)
    grad_attn = dot_nn(grad_middle_low[:, :half], proj_t[0]) + dot_nn(grad_middle_low[:, half:], proj_t[1])
    grad_attn = grad_attn.astype(BF).reshape(micro, extent, QUERY_COLUMNS)
    grad_q, gk_part, gv_part, head_rows = attend_back(q_raw, kv_raw, grad_attn, q_seg, k_seg, gq, gk)
    grad_q = grad_q.reshape(rows, QUERY_COLUMNS)
    gk_all = gk_part.reshape(count * rows, KEY_COLUMNS)
    gv_all = gv_part.reshape(count * rows, KEY_COLUMNS)
    pieces = [(grad_q, normed_low), (gk_all, normed_around), (gv_all, normed_around)]
    qkv_parts = scatter_all(weight_grad(pieces, k), index)
    grad_kv = jnp.concatenate([gk_all, gv_all], axis=1).reshape(count, rows, 2 * KEY_COLUMNS)
    total_kv = to_earlier([grad_kv[i] for i in range(depth)], grad_kv[depth].astype(F32))
    total_kv = total_kv.astype(BF)
    grad_normed = dot_nn(grad_q, query_t) + dot_nn(total_kv, kv_t)
    grad_in, attn_rows = norm_back(inputs, inv_one, attn_gain, grad_normed)
    input_grad = (grad_middle + grad_in).reshape(tokens.shape)

    masters = (qkv_master, proj_master, upgate_master, down_master)
    parts = (qkv_parts, proj_parts, upgate_parts, down_parts)
    means = (qkv_mean, proj_mean, upgate_mean, down_mean)
    squares = (qkv_square, proj_square, upgate_square, down_square)
    moved = [moments(i, parts[i], means[i], squares[i], masters[i]) for i in range(4)]
    heads_row = head_rows[0:2, :HEAD_WIDTH] + head_rows[0:2, HEAD_WIDTH:]
    early_row = moved[1][4] + moved[2][4] + moved[3][4]
    early = jnp.concatenate([jnp.sum(ffn_rows, axis=0).reshape(8, 128), early_row])
    late = jnp.concatenate([jnp.sum(attn_rows, axis=0).reshape(8, 128), moved[0][4], heads_row.reshape(1, 128)])
    early, late = total_everywhere(early), total_everywhere(late)
    early_norms = jnp.sqrt(early[8])
    gain_outs, lamb_norms, ratios = finish(early, late, gain_master, gain_mean, gain_square)
    gain_grad, gain_weight, gain_first, gain_second = gain_outs
    outs = [block_out, input_grad]
    for i in range(4):
        ratio = ratios[0] if i == 0 else early_norms[i] / (early_norms[4 + i] + EPS_ADAM)
        grad, first, second, update, _ = moved[i]
        outs += [grad, masters[i] - RATE * ratio * update, first, second]
    return (*outs, gain_grad, gain_weight, gain_first, gain_second, lamb_norms)


def solution(mesh):
    n_ctx, n_wsh = mesh.devices.shape
    fine = Mesh(mesh.devices.reshape(2, 2, n_ctx // 16, 2, 2, n_wsh), EVERY)
    sequence = P("wsh", CTX)
    weight = P("wsh", CTX)
    return jax.shard_map(
        local,
        mesh=fine,
        in_specs=(sequence,) * 3 + (weight,) * 12 + (P(),) * 3,
        out_specs=(sequence,) * 2 + (weight,) * 16 + (P(),) * 5,
        check_vma=False,
    )
```

```python
import functools

import jax
import jax.numpy as jnp
from jax import lax
from jax.experimental import pallas as pl
from jax.experimental.pallas import tpu as pltpu
from jax.sharding import Mesh
from jax.sharding import PartitionSpec as P


D = 1024
QUERY_HEADS = 16
KEY_VALUE_HEADS = 8
HEAD_WIDTH = 64
STEP = 10
GAINS = 2176
QUERY_COLUMNS = QUERY_HEADS * HEAD_WIDTH
KEY_COLUMNS = KEY_VALUE_HEADS * HEAD_WIDTH
PAIR = 2 * HEAD_WIDTH
N_PAIRS = KEY_VALUE_HEADS // 2

EPS_NORM = 1e-05
BETA_ONE = 0.9
BETA_TWO = 0.999
EPS_ADAM = 1e-06
DECAY = 0.01
RATE = 0.5
NEGATIVE_FILLER = -1e30

FAR = ("hi", "top", "low")
CTX = (*FAR, "near", "core")
QUARTERS = ("hi", "top")
EVERY = (*CTX, "wsh")
OTHERS = ("hi", "wsh", "low", "near")

BF = jnp.bfloat16
F32 = jnp.float32


def swap(block, axis):
    return lax.ppermute(block, axis, [(0, 1), (1, 0)])


def from_earlier(package, depth):
    here, quarter, n, k = (lax.axis_index(a) for a in (CTX, QUARTERS, "near", "core"))
    if lax.axis_size("low") > 1:
        size = lax.axis_size(CTX)
        blocks, exists = [], []
        for distance in range(1, depth + 1):
            route = [(i - distance, i) for i in range(distance, size)]
            blocks.append(lax.ppermute(package, CTX, route))
            exists.append(here >= distance)
        return blocks, exists
    before = lax.ppermute(package, QUARTERS, [(0, 1), (1, 2), (2, 3)])
    across = swap(jnp.where(n == 0, package, before), "near")
    beside = swap(jnp.where(k == 0, package, before), "core")
    diagonal = swap(across, "core")
    later = quarter > 0
    return [before, across, beside, diagonal], [later, later | (n == 1), later | (k == 1), later | (n == 1)]


def to_earlier(parts, own):
    n, k = lax.axis_index("near"), lax.axis_index("core")
    if lax.axis_size("low") > 1:
        size = lax.axis_size(CTX)
        for distance, part in enumerate(parts, 1):
            route = [(i, i - distance) for i in range(distance, size)]
            own = own + lax.ppermute(part, CTX, route).astype(F32)
        return own
    before, across, beside, diagonal = parts
    beside = swap(beside, "core").astype(F32)
    diagonal = swap(diagonal, "core").astype(F32)
    across = swap((across.astype(F32) + diagonal).astype(BF), "near").astype(F32)
    before = before.astype(F32) + jnp.where(k == 1, beside, 0.0) + jnp.where(n == 1, across, 0.0)
    after = lax.ppermute(before.astype(BF), QUARTERS, [(1, 0), (2, 1), (3, 2)]).astype(F32)
    return own + jnp.where(k == 0, beside, 0.0) + jnp.where(n == 0, across, 0.0) + after


def in_order(mine, other, index, at=0):
    return jnp.where(index == 0, jnp.stack([mine, other], at), jnp.stack([other, mine], at))


def pick(array, index, axis):
    return lax.dynamic_index_in_dim(array, index, axis, keepdims=False)


def total_everywhere(block):
    for axis in ("core", "wsh", "near", "hi", "top", "low"):
        size = lax.axis_size(axis)
        step = 1
        while step < size:
            block = block + lax.ppermute(block, axis, [(i, i ^ step) for i in range(size)])
            step *= 2
    return block


def rms_norm(inputs, gain):
    inverse = lax.rsqrt(jnp.mean(inputs * inputs, axis=-1, keepdims=True) + EPS_NORM)
    return inputs * inverse * gain, inverse


def norm_back(inputs, inverse, gain, grad_out):
    weighted = grad_out * gain
    inner = jnp.mean(weighted * inputs, axis=-1, keepdims=True)
    grad_in = inverse * weighted - inputs * (inverse * inverse * inverse) * inner
    return grad_in, grad_out * inputs * inverse


def lamb_moments(grad, mean, square):
    first = BETA_ONE * mean + (1.0 - BETA_ONE) * grad
    second = BETA_TWO * square + (1.0 - BETA_TWO) * grad * grad
    bias_one = 1.0 - BETA_ONE**STEP
    bias_two = 1.0 - BETA_TWO**STEP
    direction = first / bias_one / (jnp.sqrt(second / bias_two) + EPS_ADAM)
    return first, second, direction


def low_half():
    return lax.broadcasted_iota(jnp.int32, (1, PAIR), 1) < HEAD_WIDTH


def dot_nt(a, b):
    return lax.dot_general(a, b, (((1,), (1,)), ((), ())), preferred_element_type=F32)


def dot_tn(a, b):
    return lax.dot_general(a, b, (((0,), (0,)), ((), ())), preferred_element_type=F32)


def dot_nn(a, b):
    return lax.dot_general(a, b, (((1,), (0,)), ((), ())), preferred_element_type=F32)


def half_sums(block):
    row = lax.broadcasted_iota(jnp.int32, (PAIR, PAIR), 0) < HEAD_WIDTH
    col = lax.broadcasted_iota(jnp.int32, (PAIR, PAIR), 1) < HEAD_WIDTH
    ones = jnp.where(row == col, 1.0, 0.0).astype(BF)
    high = block.astype(BF)
    rest = (block - high.astype(F32)).astype(BF)
    return dot_nn(high, ones) + dot_nn(rest, ones)


def head_norm(block, gain):
    inverse = lax.rsqrt(half_sums(block * block) * (1.0 / HEAD_WIDTH) + EPS_NORM)
    return block * inverse * gain, inverse


def head_norm_back(raw, inverse, gain, grad):
    weighted = grad * gain
    inner = half_sums(weighted * raw) * (1.0 / HEAD_WIDTH)
    return inverse * weighted - raw * (inverse * inverse * inverse) * inner


def spread(block):
    low = low_half()
    turned = pltpu.roll(block, HEAD_WIDTH, 1)
    return jnp.where(low, block, turned).astype(BF), jnp.where(low, turned, block).astype(BF)


def stacked(block):
    low = low_half()
    return jnp.concatenate([jnp.where(low, block, 0.0), jnp.where(low, 0.0, block)], axis=0).astype(BF)


def unstacked(block):
    rows = block.shape[0] // 2
    return jnp.where(low_half(), block[:rows], block[rows:])


def allowed_mask(q_seg, k_seg):
    rows = q_seg.shape[1]
    behind = (k_seg.shape[0] - 1) * rows
    columns = [jnp.broadcast_to(k_seg[i : i + 1], (rows, rows)).T for i in range(k_seg.shape[0])]
    k_column = jnp.concatenate(columns, axis=0)
    key = lax.broadcasted_iota(jnp.int32, k_column.shape, 0)
    query = lax.broadcasted_iota(jnp.int32, k_column.shape, 1)
    mask = (k_column == q_seg) & (key <= query + behind)
    return jnp.concatenate([mask, mask], axis=1)


def joined(ref):
    return ref[:, 0].reshape(-1, ref.shape[3])


def softmax_parts(scores, mask):
    filled = jnp.where(mask, scores, NEGATIVE_FILLER)
    top = jnp.max(filled, axis=0, keepdims=True)
    weights = jnp.exp(filled - top)
    return weights, 1.0 / jnp.sum(weights, axis=0, keepdims=True)


def forward_kernel(q_ref, k_ref, v_ref, qs_ref, ks_ref, gq_ref, gk_ref, o_ref):
    mask = allowed_mask(qs_ref[0], ks_ref[0])
    key_pair = spread(head_norm(joined(k_ref), gk_ref[...])[0])
    value_pair = spread(joined(v_ref))
    for head in range(2):
        at = pl.ds(head * PAIR, PAIR)
        query = head_norm(q_ref[0, :, at], gq_ref[...])[0].astype(BF).astype(F32)
        scores = dot_nt(key_pair[head], stacked(query * HEAD_WIDTH**-0.5))
        weights, inverse = softmax_parts(scores, mask)
        attended = dot_tn(value_pair[head], weights.astype(BF)) * inverse
        o_ref[0, :, at] = unstacked(attended.T).astype(BF)


def backward_kernel(
    q_ref, k_ref, v_ref, go_ref, qs_ref, ks_ref, gq_ref, gk_ref, gq_out, gk_out, gv_out, gain_out
):
    mask = allowed_mask(qs_ref[0], ks_ref[0])
    raw_key = joined(k_ref)
    normed_key, inverse_key = head_norm(raw_key, gk_ref[...])
    key_pair = spread(normed_key)
    value_pair = spread(joined(v_ref))
    low = low_half()
    shape = (k_ref.shape[0], *k_ref.shape[2:])

    @pl.when((pl.program_id(0) == 0) & (pl.program_id(1) == 0))
    def _():
        gain_out[...] = jnp.zeros_like(gain_out)

    grad_keys, grad_values = [], []
    for head in range(2):
        at = pl.ds(head * PAIR, PAIR)
        raw = q_ref[0, :, at]
        normed, inverse_norm = head_norm(raw, gq_ref[...])
        query = stacked(normed.astype(BF).astype(F32) * HEAD_WIDTH**-0.5)
        weights, inverse = softmax_parts(dot_nt(key_pair[head], query), mask)
        probs = weights * inverse
        grad_out = stacked(go_ref[0, :, at].astype(F32))
        grad_probs = dot_nt(value_pair[head], grad_out)
        delta = jnp.sum(probs * grad_probs, axis=0, keepdims=True)
        grad_scores = (probs * (grad_probs - delta)).astype(BF)
        grad_query = unstacked(dot_tn(key_pair[head], grad_scores).T) * HEAD_WIDTH**-0.5
        key_part = dot_nn(grad_scores, query)
        value_part = dot_nn(probs.astype(BF), grad_out)
        grad_keys.append(key_part + pltpu.roll(key_part, HEAD_WIDTH, 1))
        grad_values.append(value_part + pltpu.roll(value_part, HEAD_WIDTH, 1))
        gq_out[0, :, at] = head_norm_back(raw, inverse_norm, gq_ref[...], grad_query).astype(BF)
        gain_out[0:1, :] += jnp.sum(grad_query * raw * inverse_norm, axis=0, keepdims=True)
    grad_key = jnp.where(low, grad_keys[0], grad_keys[1])
    gain_out[1:2, :] += jnp.sum(grad_key * raw_key * inverse_key, axis=0, keepdims=True)
    gk_out[:, 0] = head_norm_back(raw_key, inverse_key, gk_ref[...], grad_key).astype(BF).reshape(shape)
    gv_out[:, 0] = jnp.where(low, grad_values[0], grad_values[1]).astype(BF).reshape(shape)


def attention_specs(rows, count):
    q_spec = pl.BlockSpec((1, rows, 2 * PAIR), lambda s, p: (s, 0, p))
    k_spec = pl.BlockSpec((count, 1, rows, PAIR), lambda s, p: (0, s, 0, p))
    v_spec = pl.BlockSpec((count, 1, rows, PAIR), lambda s, p: (0, s, 0, N_PAIRS + p))
    qs_spec = pl.BlockSpec((1, 1, rows), lambda s, p: (s, 0, 0))
    ks_spec = pl.BlockSpec((1, count, rows), lambda s, p: (s, 0, 0))
    gain_spec = pl.BlockSpec((1, PAIR), lambda s, p: (0, 0))
    return q_spec, k_spec, v_spec, qs_spec, ks_spec, gain_spec


def attention_cost(micro, rows, keys, products):
    work = micro * QUERY_HEADS * rows * keys
    return pl.CostEstimate(
        flops=2 * 4 * PAIR * products * work,
        bytes_accessed=micro * (rows * 6 * QUERY_COLUMNS + keys * 8 * KEY_COLUMNS),
        transcendentals=work,
    )


def attend(q, kv, q_seg, k_seg, gq, gk):
    count, micro, rows, _ = kv.shape
    q_spec, k_spec, v_spec, qs_spec, ks_spec, gain_spec = attention_specs(rows, count)
    return pl.pallas_call(
        forward_kernel,
        grid=(micro, N_PAIRS),
        in_specs=[q_spec, k_spec, v_spec, qs_spec, ks_spec, gain_spec, gain_spec],
        out_specs=q_spec,
        out_shape=jax.ShapeDtypeStruct((micro, rows, QUERY_COLUMNS), BF),
        cost_estimate=attention_cost(micro, rows, count * rows, 2),
        name="attend",
    )(q, kv, kv, q_seg, k_seg, gq, gk)


def attend_back(q, kv, grad_out, q_seg, k_seg, gq, gk):
    count, micro, rows, _ = kv.shape
    q_spec, k_spec, v_spec, qs_spec, ks_spec, gain_spec = attention_specs(rows, count)
    part = jax.ShapeDtypeStruct((count, micro, rows, KEY_COLUMNS), BF)
    return pl.pallas_call(
        backward_kernel,
        grid=(micro, N_PAIRS),
        in_specs=[q_spec, k_spec, v_spec, q_spec, qs_spec, ks_spec, gain_spec, gain_spec],
        out_specs=[q_spec, k_spec, k_spec, pl.BlockSpec((8, PAIR), lambda s, p: (0, 0))],
        out_shape=[
            jax.ShapeDtypeStruct((micro, rows, QUERY_COLUMNS), BF),
            part,
            part,
            jax.ShapeDtypeStruct((8, PAIR), F32),
        ],
        cost_estimate=attention_cost(micro, rows, count * rows, 5),
        name="attend_back",
    )(q, kv, kv, grad_out, q_seg, k_seg, gq, gk)


def far_blocks(block):
    size, me = lax.axis_size(FAR), lax.axis_index(FAR)
    if size > 4:
        return lax.all_gather(block, FAR, axis=0, tiled=False)
    found = [block]
    for distance in range(1, size):
        found.append(lax.ppermute(block, FAR, [(i, (i + distance) % size) for i in range(size)]))
    ordered = []
    for at in range(size):
        offset = (me - at) % size
        chosen = found[0]
        for distance in range(1, size):
            chosen = jnp.where(offset == distance, found[distance], chosen)
        ordered.append(chosen)
    return jnp.stack(ordered)


def far_parts(blocks):
    size, me = lax.axis_size(FAR), lax.axis_index(FAR)
    if size > 4:
        return [lax.psum_scatter(blocks, FAR, scatter_dimension=0, tiled=True)[0]]
    found = [pick(blocks, me, 0)]
    for distance in range(1, size):
        leaving = pick(blocks, (me + distance) % size, 0)
        found.append(lax.ppermute(leaving, FAR, [(i, (i + distance) % size) for i in range(size)]))
    return found


def exchange_sum(blocks, axis, index, at):
    other = swap(pick(blocks, 1 - index, at), axis)
    return (pick(blocks, index, at).astype(F32) + other.astype(F32)).astype(BF)


def lane_half(block, index):
    half = block.shape[-1] // 2
    return jnp.where(index == 0, block[..., :half], block[..., half:])


def exchange_lanes_sum(blocks, index):
    other = swap(lane_half(blocks, 1 - index), "wsh")
    return (lane_half(blocks, index).astype(F32) + other.astype(F32)).astype(BF)


def exchange(block, axis, index, at):
    return in_order(block, swap(block, axis), index, at)


def interleave_kernel(k_ref, mine_ref, other_ref, *outs):
    is_mine = pl.program_id(0) == k_ref[0]
    start = 0
    for out in outs:
        at = pl.ds(start, out.shape[2])
        start += out.shape[2]

        @pl.when(is_mine)
        def _(out=out, at=at):
            out[:, 0] = mine_ref[:, at, :]

        @pl.when(jnp.logical_not(is_mine))
        def _(out=out, at=at):
            out[:, 0] = other_ref[:, at, :]


def interleave(mine, other, k, widths):
    columns = mine.shape[-1]
    mine, other = (v.reshape(-1, sum(widths), columns) for v in (mine, other))
    count = mine.shape[0]
    whole = pl.BlockSpec(mine.shape, lambda c, _: (0, 0, 0))
    outs = pl.pallas_call(
        interleave_kernel,
        grid_spec=pltpu.PrefetchScalarGridSpec(
            num_scalar_prefetch=1,
            grid=(2,),
            in_specs=[whole, whole],
            out_specs=[pl.BlockSpec((count, 1, width, columns), lambda c, _: (0, c, 0, 0)) for width in widths],
        ),
        out_shape=[jax.ShapeDtypeStruct((count, 2, width, columns), BF) for width in widths],
        cost_estimate=pl.CostEstimate(flops=0, bytes_accessed=8 * mine.size, transcendentals=0),
        name="interleave",
    )(k.reshape(1).astype(jnp.int32), mine, other)
    return [v.reshape(-1, columns) for v in outs]


def gather_all(shards, index):
    n, k, w = index
    widths = [shard.shape[1] for shard in shards]
    part = far_blocks(jnp.concatenate([shard.astype(BF).T for shard in shards]))
    cut = part.shape[0] // 2
    one = exchange(part[:cut], "near", n, 1)
    two = exchange_lanes(part[cut:], w)
    one = exchange_lanes(one, w)
    two = exchange(two, "near", n, 1)
    firsts = interleave(one, swap(one, "core"), k, widths)
    seconds = interleave(two, swap(two, "core"), k, widths)
    return [half for pair in zip(firsts, seconds) for half in pair]


def grad_kernel(firsts, k_ref, *refs):
    groups = len(firsts) - 1
    keep, leave = refs[2 * groups :]
    chips, width, _ = keep.shape
    for i in range(groups):

        @pl.when((pl.program_id(0) >= firsts[i]) & (pl.program_id(0) < firsts[i + 1]))
        def _(i=i):
            whole = dot_tn(refs[2 * i][...], refs[2 * i + 1][...])
            is_first = k_ref[0] == 0
            for chip in range(chips):
                at = 2 * chip * width
                first, second = whole[at : at + width], whole[at + width : at + 2 * width]
                keep[chip] = jnp.where(is_first, first, second).astype(BF)
                leave[chip] = jnp.where(is_first, second, first).astype(BF)


def weight_grad(pairs, k):
    chips = lax.axis_size(FAR) * lax.axis_size("near")
    chip_width = sum(a.shape[1] for a, _ in pairs) // chips
    step = min(512, *(a.shape[1] for a, _ in pairs))
    if chip_width % 128 or step % chip_width:
        whole = jnp.concatenate([dot_tn(a, b).astype(BF) for a, b in pairs])
        whole = whole.reshape(chips, 2, chip_width // 2, -1)
        return pick(whole, k, 1), pick(whole, 1 - k, 1)
    firsts, specs, operands = [0], [], []
    for a, b in pairs:
        start, count = firsts[-1], a.shape[1] // step
        block = pl.BlockSpec((a.shape[0], step), lambda i, _, s=start, c=count: (0, jnp.clip(i - s, 0, c - 1)))
        specs += [block, pl.BlockSpec(b.shape, lambda i, _: (0, 0))]
        operands += [a, b]
        firsts.append(start + count)
    columns = pairs[0][1].shape[1]
    out = pl.BlockSpec((step // chip_width, chip_width // 2, columns), lambda i, _: (i, 0, 0))
    shape = jax.ShapeDtypeStruct((chips, chip_width // 2, columns), BF)
    return pl.pallas_call(
        functools.partial(grad_kernel, tuple(firsts)),
        grid_spec=pltpu.PrefetchScalarGridSpec(
            num_scalar_prefetch=1, grid=(firsts[-1],), in_specs=specs, out_specs=[out, out]
        ),
        out_shape=[shape, shape],
        cost_estimate=pl.CostEstimate(
            flops=sum(2 * a.shape[0] * a.shape[1] * columns for a, _ in pairs),
            bytes_accessed=2 * sum(a.size + b.size for a, b in pairs) + 4 * chips * chip_width * columns,
            transcendentals=0,
        ),
        name="weight_grad",
    )(k.reshape(1).astype(jnp.int32), *operands)


def scatter_all(grads, index):
    n, _, w = index
    keep, leave = grads
    far = lax.axis_size(FAR)
    cut = far // 2
    part = (keep.astype(F32) + swap(leave, "core").astype(F32)).astype(BF)
    part = part.reshape(far, 2, *part.shape[1:])
    one = exchange_sum(part[:cut], "near", n, 1)
    two = exchange_lanes_sum(part[cut:], w)
    one = exchange_lanes_sum(one, w)
    two = exchange_sum(two, "near", n, 1)
    return far_parts(jnp.concatenate([one, two]))


def exchange_lanes(block, index):
    other = swap(block, "wsh")
    first = jnp.concatenate([block, other], axis=-1)
    return jnp.where(index == 0, first, jnp.concatenate([other, block], axis=-1))


def gather_upgate(shard):
    whole = lax.all_gather(shard.astype(BF).T, OTHERS, axis=0, tiled=False)
    whole = whole.reshape(2, 2, -1, shard.shape[0])
    return [jnp.concatenate([whole[i, 0], whole[i, 1]], axis=1) for i in range(2)]


def scatter_upgate(grad_gate, grad_upper, tokens):
    half = D // 2
    halves = (tokens[:, :half], tokens[:, half:])
    blocks = jnp.stack([dot_tn(a, b).astype(BF) for a in (grad_gate, grad_upper) for b in halves])
    blocks = blocks.reshape(2 * lax.axis_size(OTHERS) // 2, -1, half)
    return [lax.psum_scatter(blocks, OTHERS, scatter_dimension=0, tiled=True)[0]]


CROSS = ((0, 0), (1, 2), (2, 1), (3, 3))


def cross(block):
    return lax.ppermute(block, ("top", "wsh"), CROSS)


def gather_down(shard, k):
    rows, width = shard.shape
    low = lax.axis_size("low")
    parts = cross(shard.astype(BF).T).reshape(width, 2 * low, 2, rows // (4 * low))
    both = in_order(pick(parts, k, 2), swap(pick(parts, 1 - k, 2), "core"), k)
    both = both.reshape(2 * width, rows // 2)
    return lax.all_gather(both, OTHERS, axis=0, tiled=True)


def scatter_down(grad, k):
    total = grad.shape[1]
    low = lax.axis_size("low")
    blocks = grad.reshape(lax.axis_size(OTHERS), -1, total)
    part = lax.psum_scatter(blocks, OTHERS, scatter_dimension=0, tiled=True)[0]
    width = part.shape[0] // 2
    parts = part.reshape(2, width, 2 * low, total // (2 * low))
    both = in_order(pick(parts, k, 0), swap(pick(parts, 1 - k, 0), "core"), k)
    return [cross(both.transpose(1, 2, 0, 3).reshape(width, 2 * total))]


def four_tokens(block):
    across = swap(block, "top")
    return jnp.concatenate([block, swap(block, "core"), across, swap(across, "core")])


def four_sum(partial):
    rows = partial.shape[0] // 4
    leaving = jnp.concatenate([partial[3 * rows :], partial[rows : 2 * rows]]).astype(BF)
    other = swap(leaving, "core").astype(F32)
    across = swap((partial[2 * rows : 3 * rows] + other[:rows]).astype(BF), "top")
    return partial[:rows] + other[rows:] + across.astype(F32)


def finish_kernel(total_ref, m_ref, mean_ref, sq_ref, g_out, w_out, f_out, s_out, n_out, r_out):
    row = lax.broadcasted_iota(jnp.int32, (17, 128), 0)
    lane = lax.broadcasted_iota(jnp.int32, (17, 128), 1)
    grad = total_ref[0:17, :]
    first, second, update = lamb_moments(grad, mean_ref[...], sq_ref[...])
    g_out[...] = grad
    f_out[...] = first
    s_out[...] = second
    master = m_ref[...]
    squares = total_ref[17:18, :]
    at = lax.broadcasted_iota(jnp.int32, (1, 128), 1)
    segment = jnp.where(row < 8, 0, jnp.where(row < 16, 1, jnp.where(lane < HEAD_WIDTH, 2, 3)))
    spot_row = lax.broadcasted_iota(jnp.int32, (2, 8), 0)
    spot_col = lax.broadcasted_iota(jnp.int32, (2, 8), 1)
    norms = jnp.zeros((2, 8), F32)
    ratio_lane = jnp.zeros((1, 128), F32)
    ratio_gain = jnp.zeros((17, 128), F32)
    for i in range(8):
        if i < 4:
            weight_sq = jnp.sum(jnp.where(at == i, squares, 0.0), keepdims=True)
            update_sq = jnp.sum(jnp.where(at == 4 + i, squares, 0.0), keepdims=True)
        else:
            weight_sq = jnp.sum(jnp.where(segment == i - 4, master * master, 0.0), keepdims=True)
            update_sq = jnp.sum(jnp.where(segment == i - 4, update * update, 0.0), keepdims=True)
        weight_norm, update_norm = jnp.sqrt(weight_sq), jnp.sqrt(update_sq)
        ratio = weight_norm / (update_norm + EPS_ADAM)
        norms = jnp.where(spot_col == i, jnp.where(spot_row == 0, weight_norm, update_norm), norms)
        if i < 4:
            ratio_lane = jnp.where(at == i, ratio, ratio_lane)
        else:
            ratio_gain = jnp.where(segment == i - 4, ratio, ratio_gain)
    n_out[...] = norms
    r_out[...] = ratio_lane
    w_out[...] = master - RATE * ratio_gain * update


def finish(total, master, mean, square):
    shaped = [v.reshape(17, 128) for v in (master, mean, square)]
    plane = jax.ShapeDtypeStruct((17, 128), F32)
    *gains, norms, ratios = pl.pallas_call(
        finish_kernel,
        out_shape=[plane] * 4 + [jax.ShapeDtypeStruct((2, 8), F32), jax.ShapeDtypeStruct((1, 128), F32)],
        name="finish",
    )(total, *shaped)
    return [g.reshape(GAINS) for g in gains], norms, ratios[0]


def moments_kernel(which, steps, count, turn, *refs):
    parts = refs[:count]
    m_ref, s_ref, w_ref, g_out, f_out, s_out, u_out, sum_out, acc = refs[count:]
    step = pl.program_id(0)

    @pl.when(step == 0)
    def _():
        acc[...] = jnp.zeros_like(acc)

    grad = parts[0][...].astype(F32)
    for part in parts[1:]:
        grad += part[...].astype(F32)
    if turn:
        grad = grad.T
    master = w_ref[...]
    first, second, direction = lamb_moments(grad, m_ref[...], s_ref[...])
    update = direction + DECAY * master
    g_out[...] = grad
    f_out[...] = first
    s_out[...] = second
    u_out[...] = update
    acc[0:1, :] += jnp.sum(master * master, axis=0, keepdims=True)
    acc[1:2, :] += jnp.sum(update * update, axis=0, keepdims=True)

    @pl.when(step == steps - 1)
    def _():
        lane = lax.broadcasted_iota(jnp.int32, (1, 128), 1)
        master_sum = jnp.sum(acc[0:1, :], keepdims=True)
        update_sum = jnp.sum(acc[1:2, :], keepdims=True)
        sum_out[...] = jnp.where(lane == which, master_sum, jnp.where(lane == 4 + which, update_sum, 0.0))


def moments(which, parts, mean, square, master):
    rows, columns = master.shape
    turn = columns % 128 == 0
    steps = 4 if rows % 512 == 0 else 6
    if rows % (128 * steps):
        steps = 1
    tall = pl.BlockSpec((columns, rows // steps), lambda i: (0, i))
    block = pl.BlockSpec((rows // steps, columns), lambda i: (i, 0)) if turn else tall
    others = (mean, square, master) if turn else (mean.T, square.T, master.T)
    plane = jax.ShapeDtypeStruct(others[0].shape, F32)
    *outs, sums = pl.pallas_call(
        functools.partial(moments_kernel, which, steps, len(parts), turn),
        grid=(steps,),
        in_specs=[tall] * len(parts) + [block] * 3,
        out_specs=[block] * 4 + [pl.BlockSpec((1, 128), lambda i: (0, 0))],
        out_shape=[plane] * 4 + [jax.ShapeDtypeStruct((1, 128), F32)],
        scratch_shapes=[pltpu.VMEM((2, block.block_shape[1]), F32)],
        cost_estimate=pl.CostEstimate(
            flops=20 * rows * columns, bytes_accessed=32 * rows * columns, transcendentals=2 * rows * columns
        ),
        name="moments",
    )(*parts, *others)
    return *(outs if turn else [o.T for o in outs]), sums


def local(
    tokens, segment_ids, cotangent,
    qkv_master, qkv_mean, qkv_square,
    proj_master, proj_mean, proj_square,
    upgate_master, upgate_mean, upgate_square,
    down_master, down_mean, down_square,
    gain_master, gain_mean, gain_square,
):
    micro, extent, _ = tokens.shape
    rows = micro * extent
    n_ctx = lax.axis_size(CTX)
    depth = n_ctx // 4
    n, k, w = (lax.axis_index(a) for a in ("near", "core", "wsh"))
    index = (n, k, w)
    half = D // 2
    attn_gain = gain_master[:D]
    ffn_gain = gain_master[D : 2 * D]
    query_gain = gain_master[2 * D : 2 * D + HEAD_WIDTH]
    key_gain = gain_master[2 * D + HEAD_WIDTH :]
    gq = jnp.tile(query_gain, 2)[None]
    gk = jnp.tile(key_gain, 2)[None]

    extra = jnp.pad(segment_ids.astype(BF).reshape(1, rows), ((0, 15), (0, D - rows)))
    package = jnp.concatenate([tokens.reshape(rows, D), extra])
    halo, exists = from_earlier(package, depth)
    query_t, kv_t, *proj_t = gather_all((qkv_master, proj_master), index)
    gate_t, up_t = gather_upgate(upgate_master)
    down_t = gather_down(down_master, k)

    count = depth + 1
    around = jnp.concatenate([came[:rows] for came in halo] + [package[:rows]]).astype(F32)
    seg_rows = jnp.concatenate([came[rows : rows + 1, :rows] for came in halo] + [package[rows : rows + 1, :rows]])
    row = lax.broadcasted_iota(jnp.int32, (count, rows), 0)
    present = row == depth
    for i, there in enumerate(exists):
        present = present | ((row == i) & there)
    k_seg = jnp.where(present, seg_rows.astype(F32), -1.0).reshape(count, micro, extent).transpose(1, 0, 2)
    q_seg = segment_ids[:, None, :].astype(F32)
    normed_around = lax.optimization_barrier(rms_norm(around, attn_gain)[0].astype(BF))
    inputs = tokens.astype(F32).reshape(rows, D)
    inv_one = lax.rsqrt(jnp.mean(inputs * inputs, axis=-1, keepdims=True) + EPS_NORM)
    normed_low = normed_around[depth * rows :]
    q_raw = dot_nt(normed_low, query_t).reshape(micro, extent, QUERY_COLUMNS)
    kv_raw = dot_nt(normed_around, kv_t).reshape(count, micro, extent, 2 * KEY_COLUMNS)
    attn_low = attend(q_raw, kv_raw, q_seg, k_seg, gq, gk).reshape(rows, QUERY_COLUMNS)

    cot_low = cotangent.reshape(rows, D)
    cot_four = four_tokens(cot_low)
    middle = inputs + jnp.concatenate([dot_nt(attn_low, p) for p in proj_t], axis=1)
    normed_two, inv_two = rms_norm(middle, ffn_gain)
    two_four = four_tokens(normed_two.astype(BF))
    gate = dot_nt(two_four, gate_t)
    upper = dot_nt(two_four, up_t)
    grad_hidden = dot_nn(cot_four, down_t)
    sigmoid_gate = jax.nn.sigmoid(gate)
    activated = gate * sigmoid_gate
    hidden_low = (activated * upper).astype(BF)
    grad_gate = (grad_hidden * upper * sigmoid_gate * (1.0 + gate * (1.0 - sigmoid_gate))).astype(BF)
    grad_upper = (grad_hidden * activated).astype(BF)
    grad_two_part = dot_nn(grad_gate, gate_t) + dot_nn(grad_upper, up_t)
    grad_two = four_sum(grad_two_part)
    upgate_parts = scatter_upgate(grad_gate, grad_upper, two_four)
    down_parts = scatter_down(dot_tn(cot_four, hidden_low).astype(BF), k)
    out_part = dot_nt(hidden_low, down_t)
    block_out = (lax.optimization_barrier(middle) + four_sum(out_part)).astype(BF).reshape(tokens.shape)

    grad_middle, ffn_rows = norm_back(middle, inv_two, ffn_gain, grad_two)
    grad_middle = grad_middle + cot_low.astype(F32)
    grad_middle_low = grad_middle.astype(BF)
    proj_parts = scatter_all(weight_grad([(grad_middle_low, attn_low)], k), index)
    grad_attn = dot_nn(grad_middle_low[:, :half], proj_t[0]) + dot_nn(grad_middle_low[:, half:], proj_t[1])
    grad_attn = grad_attn.astype(BF).reshape(micro, extent, QUERY_COLUMNS)
    grad_q, gk_part, gv_part, head_rows = attend_back(q_raw, kv_raw, grad_attn, q_seg, k_seg, gq, gk)
    grad_q = grad_q.reshape(rows, QUERY_COLUMNS)
    gk_all = gk_part.reshape(count * rows, KEY_COLUMNS)
    gv_all = gv_part.reshape(count * rows, KEY_COLUMNS)
    pieces = [(grad_q, normed_low), (gk_all, normed_around), (gv_all, normed_around)]
    qkv_parts = scatter_all(weight_grad(pieces, k), index)
    grad_kv = jnp.concatenate([gk_all, gv_all], axis=1).reshape(count, rows, 2 * KEY_COLUMNS)
    total_kv = to_earlier([grad_kv[i] for i in range(depth)], grad_kv[depth].astype(F32))
    total_kv = total_kv.astype(BF)
    grad_normed = dot_nn(grad_q, query_t) + dot_nn(total_kv, kv_t)
    grad_in, attn_rows = norm_back(inputs, inv_one, attn_gain, grad_normed)
    input_grad = (grad_middle + grad_in).reshape(tokens.shape)

    masters = (qkv_master, proj_master, upgate_master, down_master)
    parts = (qkv_parts, proj_parts, upgate_parts, down_parts)
    means = (qkv_mean, proj_mean, upgate_mean, down_mean)
    squares = (qkv_square, proj_square, upgate_square, down_square)
    moved = []
    for i in range(4):
        moved.append(moments(i, parts[i], means[i], squares[i], masters[i]))
    heads_row = head_rows[0:2, :HEAD_WIDTH] + head_rows[0:2, HEAD_WIDTH:]
    sums_row = moved[0][4] + moved[1][4] + moved[2][4] + moved[3][4]
    gain_rows = jnp.concatenate([jnp.sum(attn_rows, axis=0), jnp.sum(ffn_rows, axis=0)]).reshape(16, 128)
    total = total_everywhere(jnp.concatenate([gain_rows, heads_row.reshape(1, 128), sums_row]))
    gain_outs, lamb_norms, ratios = finish(total, gain_master, gain_mean, gain_square)
    gain_grad, gain_weight, gain_first, gain_second = gain_outs
    outs = [block_out, input_grad]
    for i in range(4):
        grad, first, second, update, _ = moved[i]
        outs += [grad, masters[i] - RATE * ratios[i] * update, first, second]
    return (*outs, gain_grad, gain_weight, gain_first, gain_second, lamb_norms)


def solution(mesh):
    n_ctx, n_wsh = mesh.devices.shape
    fine = Mesh(mesh.devices.reshape(2, 2, n_ctx // 16, 2, 2, n_wsh), EVERY)
    sequence = P("wsh", CTX)
    weight = P("wsh", CTX)
    return jax.shard_map(
        local,
        mesh=fine,
        in_specs=(sequence,) * 3 + (weight,) * 12 + (P(),) * 3,
        out_specs=(sequence,) * 2 + (weight,) * 16 + (P(),) * 5,
        check_vma=False,
    )
```
